512 devices in a mesh: req: 128 (over z_hi, x, y), tp: 4 (over z_lo, core).
Axes of the slice: x: 4, y: 8, z: 8 (z_hi: 4, z_lo: 2; z = z_hi * 2 + z_lo), core: 2. Of those that a mesh axis runs over, the one named last changes fastest.
Arguments:
- queries: bfloat16 [2, 1024, 2304], P(None, 'req', 'tp'), may hold values from -10 to 10
- new_keys: bfloat16 [2, 1024, 2304], P(None, 'req', 'tp'), may hold values from -4 to 4
- new_values: bfloat16 [2, 1024, 2304], P(None, 'req', 'tp'), may hold values from -4 to 4
- cache_keys: bfloat16 [32768, 2304], P('req', 'tp'), may hold values from -10 to 10
- cache_values: bfloat16 [32768, 2304], P('req', 'tp'), may hold values from -4 to 4
- lengths: int32 [128, 16], P('req'), may hold values from 1 to 128, 256 in all within a row
- hidden: bfloat16 [2, 1024, 2304], P(None, 'req'), may hold values from -6 to 6
- gain: float32 [2304], replicated, may hold values from 0.5 to 1.5
- expert_ids: int32 [2, 1024, 2], P(None, 'req'), may hold values from 0 to 7, all different within a row; in each aligned block of 8 rows (0 to 7, 8 to 15, ..., all dimensions but the last counted through in order) at most 3 rows name the same one
- route_weights: float32 [2, 1024, 2], P(None, 'req'), may hold values from 0.2 to 1
- old_place: int32 [128], replicated, may hold values from 0 to 63, as said below
- new_place: int32 [128], replicated, may hold values from 0 to 63, as said below
- old_weights: bfloat16 [128, 2304, 1728], P('req', None, 'tp'), as said below
Outputs:
- context: bfloat16 [2, 1024, 2304], P(None, 'req', 'tp')
- layer_out: bfloat16 [2, 1024, 2304], P(None, 'req', 'tp')
- new_weights: bfloat16 [128, 2304, 1728], P('req', None, 'tp')
The draws below stay inside these ranges and needn't reach their ends.
Inputs may be any that keep to these rules, and one draw needn't show every extreme that they name: `old_place`: every one of the 64 shards is held by at least one device; the others hold duplicates. `new_place`: every one of the 64 shards is held by at least one device; the others hold duplicates. `old_weights`: devices with equal old_place hold equal weights. `expert_ids`: in a batch, the 8 tokens of one device name one expert at most 3 times, and each token names distinct experts. `lengths`: each row sums to 256.
All inputs are finite; a program needn't handle non-finite values.
Results may differ from the reference program's by a relative error of at most 0.009.
Values may be sent and summed in bfloat16 or wider, within the bound.
A program may use at most 64 MiB of HBM per device.

```python
import math
import jax
import jax.numpy as jnp
import numpy as np
from jax import lax

D = 2304
HEADS = 36
HEAD_SIZE = 64
EXPERTS = 8
TOPK = 2
FFW = 4608
REQ_DEV = 8
POOL = 256
TOKENS = 1024
SPLIT = 8
SHARDS = 64
HID_DEV = 144
CAP = 3
LONGEST = 128
N_REQ = 128
N_TP = 4


def placement(key, salt):
    salted = jax.random.fold_in(key, salt)
    ordering = jax.random.permutation(jax.random.fold_in(salted, 1), N_REQ)
    extras = jax.random.randint(jax.random.fold_in(salted, 2), (N_REQ,), 0, SHARDS)
    slots = jnp.arange(N_REQ, dtype=jnp.int32)
    assigned = jnp.where(slots < SHARDS, slots, extras).astype(jnp.int32)
    return jnp.zeros((N_REQ,), jnp.int32).at[ordering].set(assigned)


def draw_queries(key, part):
    base = jnp.clip(jax.random.normal(jax.random.fold_in(key, 1), (2, TOKENS, D), jnp.float32), -4.0, 4.0)
    return base.astype(jnp.bfloat16)


def draw_cache_keys(key, part):
    base = jnp.clip(jax.random.normal(jax.random.fold_in(key, 2), (N_REQ * POOL, D), jnp.float32), -4.0, 4.0)
    return base.astype(jnp.bfloat16)


def draw_old_place(key, part):
    return placement(key, 21)


def draw_new_place(key, part):
    return placement(key, 22)


def draw_old_weights(key, part):
    holders = placement(key, 21)
    scales = jnp.array([D ** (-0.5), D ** (-0.5), FFW ** (-0.5)], jnp.float32).reshape(1, 1, 3, 1)

    def one_shard(shard_id):
        shard_key = jax.random.fold_in(jax.random.fold_in(key, 31), shard_id)
        values = jax.random.normal(shard_key, (D, N_TP, 3, HID_DEV), jnp.float32) * scales
        return values.reshape(D, N_TP * 3 * HID_DEV).astype(jnp.bfloat16)
    return lax.map(one_shard, holders)


def level_of(own_key, shape, pieces, smallest, largest):
    level = 1.0
    for axis_at, parts in pieces:
        steps = jax.random.uniform(jax.random.fold_in(jax.random.fold_in(own_key, 6), axis_at), (parts,), jnp.float32, smallest / len(pieces), largest / len(pieces))
        level = level * jnp.repeat(jnp.exp(steps), shape[axis_at] // parts).reshape((-1,) + (1,) * (len(shape) - 1 - axis_at))
    return level


def split_up(number_of, total, limit, lean):
    weights = [(1 << 20) // math.isqrt(grade ** lean) + 1 for grade in range(2, number_of + 1)]
    spare, holding = total - limit - (number_of - 1), [1] * (number_of - 1)
    while spare > 0:
        candidates = [i for i in range(number_of - 1) if holding[i] < limit]
        whole, left = sum([weights[i] for i in candidates]), spare
        for i in candidates:
            addition = min(limit - holding[i], max(1, left * weights[i] // whole), spare)
            holding[i] = holding[i] + addition
            spare = spare - addition
    return np.array([limit] + holding)


def uneven(rng, number_of, total, bound, lean):
    if number_of == 2:
        one = jax.random.randint(rng, (), max(1, total - bound), min(bound, total - 1) + 1)
        return jnp.stack([one, total - one])
    tallies = jnp.asarray(split_up(number_of, total, bound, lean), jnp.int32)
    couples = (number_of - 1) // 2
    source_of, receiver = tallies[1:1 + 2 * couples:2], tallies[2:2 + 2 * couples:2]
    margin = jnp.minimum(source_of - 1, bound - receiver)
    passed = jax.random.randint(jax.random.fold_in(rng, 1), (couples,), 0, 1 << 20) % (margin + 1)
    tallies = tallies.at[1:1 + 2 * couples:2].set(source_of - passed).at[2:2 + 2 * couples:2].set(receiver + passed)
    return tallies[jax.random.permutation(jax.random.fold_in(rng, 2), number_of)]


def routed_block(rng, own, number, rows, number_of, top, limit, skew):
    ranking = jax.random.permutation(rng, number_of)
    heavy_load, usual = load_shares(number_of, rows * top, limit, skew, True), load_shares(number_of, rows * top, limit, skew, False)
    places = jnp.arange(number_of)

    def named(sizes, offset_by):
        used = int((sizes > 0).sum())
        fixed = max(1, used // 4)
        moved = fixed + (places - fixed + offset_by * (used - fixed)) % max(1, number_of - fixed)
        return jnp.zeros((number_of,), jnp.int32).at[ranking[jnp.where(places < fixed, places, moved)]].set(jnp.asarray(sizes, jnp.int32))

    sizes = jnp.where(number % 4 == 0, named(heavy_load, number // 4), named(usual, number - number // 4 - 1))
    mixed = jax.random.permutation(jax.random.fold_in(own, 3), number_of)
    donor, taker = mixed[0:number_of // 2 * 2:2], mixed[1:number_of // 2 * 2:2]
    slack = jnp.minimum(sizes[donor] - 1, limit - sizes[taker]) // 2
    slack = jnp.where((donor == ranking[0]) | (taker == ranking[0]) | (sizes[taker] == 0), 0, jnp.maximum(slack, 0))
    moved = jax.random.randint(jax.random.fold_in(own, 4), (number_of // 2,), 0, 1 << 20) % (slack + 1)
    sizes = sizes.at[donor].add(-moved).at[taker].add(moved)
    members = jnp.searchsorted(jnp.cumsum(sizes), jnp.arange(rows * top), side="right").astype(jnp.int32)
    listing = members.reshape(top, rows).T
    listing = listing[jax.random.permutation(jax.random.fold_in(own, 1), rows)]
    offset_by = jax.random.randint(jax.random.fold_in(own, 2), (rows, 1), 0, top)
    return jnp.take_along_axis(listing, (jnp.arange(top)[None, :] + offset_by) % top, axis=1)


def load_shares(number_of, total, most, lean, full):
    portions = [(1 << 20) // math.isqrt(standing ** lean) + 1 for standing in range(1, number_of + 1)]
    largest = most if full else min(most, max(-(-total // number_of), total * portions[0] // sum(portions)))
    least = 1 if total - largest >= number_of - 1 else 0
    holding, surplus = [largest] + [least] * (number_of - 1), total - largest - least * (number_of - 1)
    while surplus > 0:
        candidates = [i for i in range(1, number_of) if holding[i] < largest] or [i for i in range(1, number_of) if holding[i] < most]
        mass, remaining = sum([portions[i] for i in candidates]), surplus
        for i in candidates:
            extra = min(most - holding[i], max(1, remaining * portions[i] // mass), surplus)
            holding[i] = holding[i] + extra
            surplus = surplus - extra
    return np.array(holding)


def bell_draw(rng, extent, width, reach, shards=(), kind=jnp.bfloat16):
    loudness = level_of(rng, extent, shards, -0.22, 0.18) if shards else 1.0
    entries = jax.random.normal(rng, extent, jnp.float32) * width * loudness
    return jnp.minimum(jnp.maximum(entries, -reach), reach).astype(kind)


def setup_inputs(seed: int = 0) -> dict:
    keys = jax.random.split(jax.random.key(seed), 14)
    queries = draw_queries(jax.random.fold_in(keys[13], 71), 0)
    new_keys = bell_draw(keys[1], (2, TOKENS, D), 1.0, 4.0, ((1, 128), (2, 4)))
    new_values = bell_draw(keys[2], (2, TOKENS, D), 1.0, 4.0, ((1, 128), (2, 4)))
    cache_keys = draw_cache_keys(jax.random.fold_in(keys[13], 71), 0)
    cache_values = bell_draw(keys[4], (N_REQ * POOL, D), 1.0, 4.0, ((0, 128), (1, 4)))
    lengths = jax.vmap(lambda own: uneven(own, 2 * REQ_DEV, POOL, LONGEST, 2))(jax.random.split(keys[5], N_REQ)).reshape((N_REQ, 2 * REQ_DEV)).astype(jnp.int32)
    hidden = bell_draw(keys[6], (2, TOKENS, D), 1.0, 6.0, ((1, 128),))
    gain = jnp.clip(1.0 + 0.1 * jax.random.normal(keys[7], (D,), jnp.float32), 0.5, 1.5)
    expert_ids_keys = jax.random.split(jax.random.fold_in(keys[8], 1), 2 * TOKENS // REQ_DEV)
    expert_ids_turns = jax.random.permutation(jax.random.fold_in(keys[8], 3), 2 * TOKENS // REQ_DEV)
    expert_ids = jax.vmap(lambda own, number: routed_block(jax.random.fold_in(keys[8], 2), own, number, REQ_DEV, EXPERTS, TOPK, CAP, 2))(expert_ids_keys, expert_ids_turns).reshape((2, TOKENS, TOPK))
    route_weights = jnp.clip(0.2 + 0.8 * jax.random.uniform(keys[9], (2, TOKENS, TOPK), jnp.float32) ** level_of(keys[9], (2, TOKENS, TOPK), ((1, 128),), -0.2, 0.2), 0.2, 1.0)
    old_place = draw_old_place(jax.random.fold_in(keys[13], 71), 0)
    new_place = draw_new_place(jax.random.fold_in(keys[13], 71), 0)
    old_weights = draw_old_weights(jax.random.fold_in(keys[13], 71), 0)
    return {"queries": queries, "new_keys": new_keys, "new_values": new_values, "cache_keys": cache_keys, "cache_values": cache_values, "lengths": lengths, "hidden": hidden, "gain": gain, "expert_ids": expert_ids, "route_weights": route_weights, "old_place": old_place, "new_place": new_place, "old_weights": old_weights}


def reference(queries, new_keys, new_values, cache_keys, cache_values, lengths, hidden, gain, expert_ids, route_weights, old_place, new_place, old_weights):
    flt = jnp.float32
    scale = HEAD_SIZE ** (-0.5)

    def to_requests(array):
        shaped = array.astype(flt).reshape(2, N_REQ, REQ_DEV, HEADS, HEAD_SIZE)
        return shaped.transpose(1, 0, 2, 3, 4).reshape(N_REQ, 2 * REQ_DEV, HEADS, HEAD_SIZE)
    query_rows = to_requests(queries)
    own_keys = to_requests(new_keys)
    own_values = to_requests(new_values)
    pool_keys = cache_keys.astype(flt).reshape(N_REQ, POOL, HEADS, HEAD_SIZE)
    pool_values = cache_values.astype(flt).reshape(N_REQ, POOL, HEADS, HEAD_SIZE)
    starts = jnp.cumsum(lengths, axis=1) - lengths
    position = jnp.arange(POOL, dtype=jnp.int32)
    owned = (position[None, None, :] >= starts[:, :, None]) & (position[None, None, :] < (starts + lengths)[:, :, None])
    scores = jnp.einsum('nqhd,nphd->nhqp', query_rows, pool_keys) * scale
    scores = jnp.where(owned[:, None], scores, -jnp.inf)
    own_score = jnp.einsum('nqhd,nqhd->nhq', query_rows, own_keys) * scale
    highest = jnp.maximum(lax.optimization_barrier(jnp.max(scores, axis=-1)), own_score)
    exp_pool = jnp.exp(scores - highest[..., None])
    exp_own = jnp.exp(own_score - highest)
    denom = lax.optimization_barrier(jnp.sum(exp_pool, axis=-1)) + exp_own
    prob_pool = lax.optimization_barrier(exp_pool.astype(jnp.bfloat16)).astype(flt)
    prob_own = lax.optimization_barrier(exp_own.astype(jnp.bfloat16)).astype(flt)
    summed = jnp.einsum('nhqp,nphd->nqhd', prob_pool, pool_values)
    summed = summed + prob_own.transpose(0, 2, 1)[..., None] * own_values
    context = (summed / denom.transpose(0, 2, 1)[..., None]).astype(jnp.bfloat16)
    context = context.reshape(N_REQ, 2, REQ_DEV, D).transpose(1, 0, 2, 3).reshape(2, TOKENS, D)
    resid = hidden.astype(flt)
    normed = (resid * gain / jnp.sqrt(lax.optimization_barrier(jnp.mean(resid * resid, axis=-1, keepdims=True)) + 1e-05)).astype(jnp.bfloat16)
    normed_f = lax.optimization_barrier(normed).astype(flt).reshape(2 * TOKENS, D)
    devices = jnp.arange(N_REQ, dtype=jnp.int32)
    shard_ids = jnp.arange(SHARDS, dtype=jnp.int32)
    first_old = lax.optimization_barrier(jnp.min(jnp.where(old_place[None, :] == shard_ids[:, None], devices[None, :], N_REQ), axis=1)).astype(jnp.int32)
    flat_ids = expert_ids.reshape(2 * TOKENS, TOPK)
    flat_weights = route_weights.reshape(2 * TOKENS, TOPK)
    coef = lax.optimization_barrier(jnp.sum(jnp.where(flat_ids[:, :, None] == jnp.arange(EXPERTS, dtype=jnp.int32)[None, None, :], flat_weights[:, :, None], 0.0), axis=1))

    def add_shard(total, shard_id):
        holder = lax.dynamic_index_in_dim(first_old, shard_id, 0, keepdims=False)
        weight_block = lax.dynamic_index_in_dim(old_weights, holder, 0, keepdims=False).astype(flt)
        weight_block = weight_block.reshape(D, N_TP, 3, HID_DEV)
        gate_out = jnp.einsum('td,dph->tph', normed_f, weight_block[:, :, 0])
        up_out = jnp.einsum('td,dph->tph', normed_f, weight_block[:, :, 1])
        act = lax.optimization_barrier((jax.nn.silu(gate_out) * up_out).astype(jnp.bfloat16)).astype(flt)
        part = jnp.einsum('tph,dph->tpd', act, weight_block[:, :, 2])
        part = lax.optimization_barrier(part.astype(jnp.bfloat16)).astype(flt)
        expert_col = lax.dynamic_slice_in_dim(coef, (shard_id // SPLIT).astype(jnp.int32), 1, 1)
        return (total + expert_col * lax.optimization_barrier(jnp.sum(part, axis=1)), None)
    total, _ = lax.scan(add_shard, jnp.zeros((2 * TOKENS, D), flt), shard_ids)
    layer_out = (resid + total.reshape(2, TOKENS, D)).astype(jnp.bfloat16)
    source = lax.optimization_barrier(jnp.sum(jnp.where(new_place[:, None] == shard_ids[None, :], first_old[None, :], 0), axis=1)).astype(jnp.int32)
    new_weights = jnp.take(old_weights, source, axis=0)
    return (context, layer_out, new_weights)
```

```python
import jax
import jax.numpy as jnp
from jax import lax
from jax.sharding import PartitionSpec as P

HEAD_SIZE = 64
EXPERTS = 8
CAP = 3


def attend(queries, new_keys, new_values, cache_keys, cache_values, lengths):
    batches, tok_rows, width = queries.shape
    heads = width // HEAD_SIZE
    pool = cache_keys.shape[0]
    scale = HEAD_SIZE ** (-0.5)
    req_lengths = lengths.reshape(-1)
    starts = jnp.cumsum(req_lengths) - req_lengths
    position = jnp.arange(pool, dtype=jnp.int32)
    owned = (position[None, :] >= starts[:, None]) & (
        position[None, :] < (starts + req_lengths)[:, None]
    )
    query_rows = queries.reshape(batches * tok_rows, heads, HEAD_SIZE)
    own_keys = new_keys.reshape(batches * tok_rows, heads, HEAD_SIZE)
    own_values = new_values.reshape(batches * tok_rows, heads, HEAD_SIZE)
    pool_keys = cache_keys.reshape(pool, heads, HEAD_SIZE)
    pool_values = cache_values.reshape(pool, heads, HEAD_SIZE)
    scores = (
        jnp.einsum("qhd,phd->hqp", query_rows, pool_keys, preferred_element_type=jnp.float32)
        * scale
    )
    scores = jnp.where(owned[None], scores, -jnp.inf)
    own_score = (
        jnp.einsum("qhd,qhd->hq", query_rows, own_keys, preferred_element_type=jnp.float32) * scale
    )
    highest = jnp.maximum(jnp.max(scores, axis=-1), own_score)
    exp_pool = jnp.exp(scores - highest[..., None])
    exp_own = jnp.exp(own_score - highest)
    denom = jnp.sum(exp_pool, axis=-1) + exp_own
    summed = jnp.einsum(
        "hqp,phd->qhd",
        exp_pool.astype(jnp.bfloat16),
        pool_values,
        preferred_element_type=jnp.float32,
    )
    prob_own = lax.optimization_barrier(exp_own.astype(jnp.bfloat16)).astype(jnp.float32)
    summed = summed + prob_own.T[:, :, None] * own_values.astype(jnp.float32)
    context = (summed / denom.T[:, :, None]).astype(jnp.bfloat16)
    return context.reshape(batches, tok_rows, width)


def expert_all(hidden, chosen, route_weights, place, shard_weights, gain):
    nreq = lax.axis_size("req")
    ntp = lax.axis_size("tp")
    me_index = lax.axis_index("req")
    split_count = max(1, nreq // 16)
    shard_count = EXPERTS * split_count
    batches, tok_rows, width = hidden.shape
    hid_dev = shard_weights.shape[1] // 3
    resid = hidden.astype(jnp.float32)
    normed = (
        resid * gain / jnp.sqrt(jnp.mean(resid * resid, axis=-1, keepdims=True) + 1e-05)
    ).astype(jnp.bfloat16)
    experts = jnp.arange(EXPERTS, dtype=jnp.int32)
    coef = jnp.sum(
        jnp.where(chosen[..., None] == experts, route_weights[..., None], 0.0), axis=-2
    )
    all_normed = lax.all_gather(normed, "req", axis=0, tiled=False)
    all_coef = lax.all_gather(coef, "req", axis=0, tiled=False)
    devices = jnp.arange(nreq, dtype=jnp.int32)
    shard_ids = jnp.arange(shard_count, dtype=jnp.int32)
    first_old = jnp.min(
        jnp.where(place[None, :] == shard_ids[:, None], devices[None, :], nreq), axis=1
    )
    my_shard = place[me_index]
    my_expert = my_shard // split_count
    designated = first_old[my_shard] == me_index
    column = jnp.sum(jnp.where(experts == my_expert, all_coef, 0.0), axis=-1)
    column = jnp.where(designated, column, 0.0).reshape(-1)
    rows = all_normed.reshape(-1, width)
    gate_up = jnp.dot(rows, shard_weights[:, : 2 * hid_dev], preferred_element_type=jnp.float32)
    act = (jax.nn.silu(gate_up[:, :hid_dev]) * gate_up[:, hid_dev:]).astype(jnp.bfloat16)
    part = lax.dot_general(
        act,
        shard_weights[:, 2 * hid_dev :],
        (((1,), (1,)), ((), ())),
        preferred_element_type=jnp.float32,
    ).astype(jnp.bfloat16)
    weighted = (part.astype(jnp.float32) * column[:, None]).astype(jnp.bfloat16)
    weighted = weighted.reshape(nreq, batches * tok_rows, width)
    mine = lax.psum_scatter(weighted, "req", scatter_dimension=0, tiled=True)
    mine = mine.reshape(batches * tok_rows, ntp, width // ntp)
    mine = lax.psum_scatter(mine, "tp", scatter_dimension=1, tiled=True)
    mine = mine.reshape(batches, tok_rows, width // ntp).astype(jnp.float32)
    tp_width = width // ntp
    tp_start = lax.axis_index("tp") * tp_width
    resid_share = lax.dynamic_slice_in_dim(resid, tp_start, tp_width, 2)
    return (resid_share + mine).astype(jnp.bfloat16)


def migrate(old_weights, old_place, new_place):
    nreq = lax.axis_size("req")
    shard_count = EXPERTS * max(1, nreq // 16)
    _, width, columns = old_weights.shape
    piece = width // nreq
    pieces = old_weights.reshape(nreq, piece, columns)
    spread = lax.all_to_all(pieces, "req", split_axis=0, concat_axis=0, tiled=True)
    devices = jnp.arange(nreq, dtype=jnp.int32)
    shard_ids = jnp.arange(shard_count, dtype=jnp.int32)
    first_old = jnp.min(
        jnp.where(old_place[None, :] == shard_ids[:, None], devices[None, :], nreq), axis=1
    )
    needed = jnp.sum(
        jnp.where(new_place[:, None] == shard_ids[None, :], first_old[None, :], 0), axis=1
    )
    sending = spread[needed]
    collected = lax.all_to_all(sending, "req", split_axis=0, concat_axis=0, tiled=True)
    return collected.reshape(1, width, columns)


def on_device(
    queries,
    new_keys,
    new_values,
    cache_keys,
    cache_values,
    lengths,
    hidden,
    gain,
    expert_ids,
    route_weights,
    old_place,
    new_place,
    old_weights,
):
    context = attend(queries, new_keys, new_values, cache_keys, cache_values, lengths)
    moved = migrate(old_weights, old_place, new_place)
    layer_out = expert_all(hidden, expert_ids, route_weights, old_place, old_weights[0], gain)
    return (context, layer_out, moved)


def solution(mesh):
    in_specs = (
        P(None, "req", "tp"),
        P(None, "req", "tp"),
        P(None, "req", "tp"),
        P("req", "tp"),
        P("req", "tp"),
        P("req", None),
        P(None, "req", None),
        P(),
        P(None, "req", None),
        P(None, "req", None),
        P(),
        P(),
        P("req", None, "tp"),
    )
    out_specs = (P(None, "req", "tp"), P(None, "req", "tp"), P("req", None, "tp"))
    return jax.shard_map(
        on_device, mesh=mesh, in_specs=in_specs, out_specs=out_specs, check_vma=False
    )
```

```python
import jax
import jax.numpy as jnp
from jax import lax
from jax.sharding import PartitionSpec as P

HEAD_SIZE = 64
EXPERTS = 8
CAP = 3


def attend(queries, new_keys, new_values, cache_keys, cache_values, lengths):
    batches, tok_rows, width = queries.shape
    heads = width // HEAD_SIZE
    pool = cache_keys.shape[0]
    scale = HEAD_SIZE ** (-0.5)
    req_lengths = lengths.reshape(-1)
    starts = jnp.cumsum(req_lengths) - req_lengths
    position = jnp.arange(pool, dtype=jnp.int32)
    owned = (position[None, :] >= starts[:, None]) & (
        position[None, :] < (starts + req_lengths)[:, None]
    )
    query_rows = queries.reshape(batches * tok_rows, heads, HEAD_SIZE)
    own_keys = new_keys.reshape(batches * tok_rows, heads, HEAD_SIZE)
    own_values = new_values.reshape(batches * tok_rows, heads, HEAD_SIZE)
    pool_keys = cache_keys.reshape(pool, heads, HEAD_SIZE)
    pool_values = cache_values.reshape(pool, heads, HEAD_SIZE)
    scores = (
        jnp.einsum("qhd,phd->hqp", query_rows, pool_keys, preferred_element_type=jnp.float32)
        * scale
    )
    scores = jnp.where(owned[None], scores, -jnp.inf)
    own_score = (
        jnp.einsum("qhd,qhd->hq", query_rows, own_keys, preferred_element_type=jnp.float32) * scale
    )
    highest = jnp.maximum(jnp.max(scores, axis=-1), own_score)
    exp_pool = jnp.exp(scores - highest[..., None])
    exp_own = jnp.exp(own_score - highest)
    denom = jnp.sum(exp_pool, axis=-1) + exp_own
    summed = jnp.einsum(
        "hqp,phd->qhd",
        exp_pool.astype(jnp.bfloat16),
        pool_values,
        preferred_element_type=jnp.float32,
    )
    prob_own = lax.optimization_barrier(exp_own.astype(jnp.bfloat16)).astype(jnp.float32)
    summed = summed + prob_own.T[:, :, None] * own_values.astype(jnp.float32)
    context = (summed / denom.T[:, :, None]).astype(jnp.bfloat16)
    return context.reshape(batches, tok_rows, width)


def choose_holders(place, me_index, nreq, shard_count):
    devices = jnp.arange(nreq, dtype=jnp.int32)
    holder = place[None, :] == jnp.arange(shard_count, dtype=jnp.int32)[:, None]
    before = (place[:, None] == place[None, :]) & (devices[:, None] < devices[None, :])
    rank_in = jnp.sum(before.astype(jnp.int32), axis=0)
    count = jnp.sum(holder.astype(jnp.int32), axis=1)
    wanted = me_index % count
    match = holder & (rank_in[None, :] == wanted[:, None])
    return jnp.sum(jnp.where(match, devices[None, :], 0), axis=1)


CORE_PAIRS = [(0, 1), (1, 0), (2, 3), (3, 2)]
Z_PAIRS = [(0, 2), (2, 0), (1, 3), (3, 1)]


def expert_routed(hidden, chosen, route_weights, place, shard_weights, gain):
    nreq = lax.axis_size("req")
    me_index = lax.axis_index("req")
    tp_index = lax.axis_index("tp")
    core = tp_index % 2
    zpos = tp_index // 2
    split_count = max(1, nreq // 16)
    shard_count = EXPERTS * split_count
    batches, tok_rows, width = hidden.shape
    slots = batches * CAP
    half = width // 2
    quarter = width // 4
    hid_dev = shard_weights.shape[1] // 3
    resid = hidden.astype(jnp.float32)
    normed = (
        resid * gain / jnp.sqrt(jnp.mean(resid * resid, axis=-1, keepdims=True) + 1e-05)
    ).astype(jnp.bfloat16)
    flat_ids = chosen.reshape(-1)
    assigns = flat_ids.shape[0]
    topk = assigns // (batches * tok_rows)
    shard_dest = choose_holders(place, me_index, nreq, shard_count)
    shard_list = flat_ids[:, None] * split_count + jnp.arange(split_count, dtype=jnp.int32)[None, :]
    pick = shard_list[:, :, None] == jnp.arange(shard_count, dtype=jnp.int32)[None, None, :]
    dest = jnp.sum(jnp.where(pick, shard_dest[None, None, :], 0), axis=-1)
    assign_index = jnp.arange(assigns, dtype=jnp.int32)
    earlier = (flat_ids[:, None] == flat_ids[None, :]) & (
        assign_index[None, :] < assign_index[:, None]
    )
    rank_in = jnp.sum(earlier.astype(jnp.int32), axis=1)
    slot = dest * slots + rank_in[:, None]
    hits = jnp.any(
        slot[None, :, :] == jnp.arange(nreq * slots, dtype=jnp.int32)[:, None, None], axis=-1
    )
    repeated = jnp.repeat(normed.reshape(batches * tok_rows, width), topk, axis=0)
    my_half = lax.dynamic_slice_in_dim(repeated, core * half, half, 1)
    outgoing = jnp.dot(hits.astype(jnp.bfloat16), my_half, preferred_element_type=jnp.float32)
    outgoing = outgoing.astype(jnp.bfloat16).reshape(nreq, slots, half)
    received = lax.all_to_all(outgoing, "req", split_axis=0, concat_axis=0, tiled=True)
    other = lax.ppermute(received, "tp", CORE_PAIRS)
    low = jnp.where(core == 0, received, other)
    high = jnp.where(core == 0, other, received)
    flat_rows = jnp.concatenate([low, high], axis=-1).reshape(nreq * slots, width)
    gate_up = jnp.dot(
        flat_rows, shard_weights[:, : 2 * hid_dev], preferred_element_type=jnp.float32
    )
    act = (jax.nn.silu(gate_up[:, :hid_dev]) * gate_up[:, hid_dev:]).astype(jnp.bfloat16)
    part = lax.dot_general(
        act,
        shard_weights[:, 2 * hid_dev :],
        (((1,), (1,)), ((), ())),
        preferred_element_type=jnp.float32,
    ).astype(jnp.bfloat16)
    part = part.reshape(nreq * slots, 2, 2, quarter)
    keep = lax.dynamic_index_in_dim(part, core, 2, keepdims=False)
    send = lax.dynamic_index_in_dim(part, 1 - core, 2, keepdims=False)
    got = lax.ppermute(send, "tp", CORE_PAIRS)
    pair_sum = (keep.astype(jnp.float32) + got.astype(jnp.float32)).astype(jnp.bfloat16)
    pair_sum = pair_sum.reshape(nreq, slots, half)
    returned = lax.all_to_all(pair_sum, "req", split_axis=0, concat_axis=0, tiled=True)
    returned = returned.reshape(nreq * slots, 2, quarter)
    picked = (
        returned[slot.reshape(-1)]
        .astype(jnp.float32)
        .reshape(batches * tok_rows, topk, split_count, 2, quarter)
    )
    weights_now = route_weights.reshape(batches * tok_rows, topk)
    partial_sum = jnp.einsum("rksze,rk->rze", picked, weights_now)
    mine = lax.dynamic_index_in_dim(partial_sum, zpos, 1, keepdims=False)
    away = lax.dynamic_index_in_dim(partial_sum, 1 - zpos, 1, keepdims=False)
    total = mine + lax.ppermute(away, "tp", Z_PAIRS)
    resid_share = lax.dynamic_slice_in_dim(resid, tp_index * quarter, quarter, 2)
    return (resid_share + total.reshape(batches, tok_rows, quarter)).astype(jnp.bfloat16)


def migrate(old_weights, old_place, new_place):
    nreq = lax.axis_size("req")
    shard_count = EXPERTS * max(1, nreq // 16)
    _, width, columns = old_weights.shape
    piece = width // nreq
    pieces = old_weights.reshape(nreq, piece, columns)
    spread = lax.all_to_all(pieces, "req", split_axis=0, concat_axis=0, tiled=True)
    devices = jnp.arange(nreq, dtype=jnp.int32)
    shard_ids = jnp.arange(shard_count, dtype=jnp.int32)
    first_old = jnp.min(
        jnp.where(old_place[None, :] == shard_ids[:, None], devices[None, :], nreq), axis=1
    )
    needed = jnp.sum(
        jnp.where(new_place[:, None] == shard_ids[None, :], first_old[None, :], 0), axis=1
    )
    sending = spread[needed]
    collected = lax.all_to_all(sending, "req", split_axis=0, concat_axis=0, tiled=True)
    return collected.reshape(1, width, columns)


def on_device(
    queries,
    new_keys,
    new_values,
    cache_keys,
    cache_values,
    lengths,
    hidden,
    gain,
    expert_ids,
    route_weights,
    old_place,
    new_place,
    old_weights,
):
    context = attend(queries, new_keys, new_values, cache_keys, cache_values, lengths)
    moved = migrate(old_weights, old_place, new_place)
    layer_out = expert_routed(hidden, expert_ids, route_weights, old_place, old_weights[0], gain)
    return (context, layer_out, moved)


def solution(mesh):
    in_specs = (
        P(None, "req", "tp"),
        P(None, "req", "tp"),
        P(None, "req", "tp"),
        P("req", "tp"),
        P("req", "tp"),
        P("req", None),
        P(None, "req", None),
        P(),
        P(None, "req", None),
        P(None, "req", None),
        P(),
        P(),
        P("req", None, "tp"),
    )
    out_specs = (P(None, "req", "tp"), P(None, "req", "tp"), P("req", None, "tp"))
    return jax.shard_map(
        on_device, mesh=mesh, in_specs=in_specs, out_specs=out_specs, check_vma=False
    )
```

```python
import jax
import jax.numpy as jnp
from jax import lax
from jax.sharding import PartitionSpec as P

HEAD_SIZE = 64
EXPERTS = 8
CAP = 3


def attend(queries, new_keys, new_values, cache_keys, cache_values, lengths):
    batches, tok_rows, width = queries.shape
    heads = width // HEAD_SIZE
    pool = cache_keys.shape[0]
    scale = HEAD_SIZE ** (-0.5)
    req_lengths = lengths.reshape(-1)
    starts = jnp.cumsum(req_lengths) - req_lengths
    position = jnp.arange(pool, dtype=jnp.int32)
    owned = (position[None, :] >= starts[:, None]) & (
        position[None, :] < (starts + req_lengths)[:, None]
    )
    query_rows = queries.reshape(batches * tok_rows, heads, HEAD_SIZE)
    own_keys = new_keys.reshape(batches * tok_rows, heads, HEAD_SIZE)
    own_values = new_values.reshape(batches * tok_rows, heads, HEAD_SIZE)
    pool_keys = cache_keys.reshape(pool, heads, HEAD_SIZE)
    pool_values = cache_values.reshape(pool, heads, HEAD_SIZE)
    scores = (
        jnp.einsum("qhd,phd->hqp", query_rows, pool_keys, preferred_element_type=jnp.float32)
        * scale
    )
    scores = jnp.where(owned[None], scores, -jnp.inf)
    own_score = (
        jnp.einsum("qhd,qhd->hq", query_rows, own_keys, preferred_element_type=jnp.float32) * scale
    )
    highest = jnp.maximum(jnp.max(scores, axis=-1), own_score)
    exp_pool = jnp.exp(scores - highest[..., None])
    exp_own = jnp.exp(own_score - highest)
    denom = jnp.sum(exp_pool, axis=-1) + exp_own
    summed = jnp.einsum(
        "hqp,phd->qhd",
        exp_pool.astype(jnp.bfloat16),
        pool_values,
        preferred_element_type=jnp.float32,
    )
    prob_own = lax.optimization_barrier(exp_own.astype(jnp.bfloat16)).astype(jnp.float32)
    summed = summed + prob_own.T[:, :, None] * own_values.astype(jnp.float32)
    context = (summed / denom.T[:, :, None]).astype(jnp.bfloat16)
    return context.reshape(batches, tok_rows, width)


def choose_holders(place, me_index, nreq, shard_count):
    devices = jnp.arange(nreq, dtype=jnp.int32)
    holder = place[None, :] == jnp.arange(shard_count, dtype=jnp.int32)[:, None]
    before = (place[:, None] == place[None, :]) & (devices[:, None] < devices[None, :])
    rank_in = jnp.sum(before.astype(jnp.int32), axis=0)
    count = jnp.sum(holder.astype(jnp.int32), axis=1)
    wanted = me_index % count
    match = holder & (rank_in[None, :] == wanted[:, None])
    return jnp.sum(jnp.where(match, devices[None, :], 0), axis=1)


CORE_PAIRS = [(0, 1), (1, 0), (2, 3), (3, 2)]
Z_PAIRS = [(0, 2), (2, 0), (1, 3), (3, 1)]


def expert_routed(hidden, chosen, route_weights, place, shard_weights, gain, extra):
    nreq = lax.axis_size("req")
    me_index = lax.axis_index("req")
    tp_index = lax.axis_index("tp")
    core = tp_index % 2
    zpos = tp_index // 2
    split_count = max(1, nreq // 16)
    shard_count = EXPERTS * split_count
    batches, tok_rows, width = hidden.shape
    slots = batches * CAP
    half = width // 2
    quarter = width // 4
    hid_dev = shard_weights.shape[1] // 3
    resid = hidden.astype(jnp.float32)
    normed = (
        resid * gain / jnp.sqrt(jnp.mean(resid * resid, axis=-1, keepdims=True) + 1e-05)
    ).astype(jnp.bfloat16)
    flat_ids = chosen.reshape(-1)
    assigns = flat_ids.shape[0]
    topk = assigns // (batches * tok_rows)
    shard_dest = choose_holders(place, me_index, nreq, shard_count)
    shard_list = flat_ids[:, None] * split_count + jnp.arange(split_count, dtype=jnp.int32)[None, :]
    pick = shard_list[:, :, None] == jnp.arange(shard_count, dtype=jnp.int32)[None, None, :]
    dest = jnp.sum(jnp.where(pick, shard_dest[None, None, :], 0), axis=-1)
    assign_index = jnp.arange(assigns, dtype=jnp.int32)
    earlier = (flat_ids[:, None] == flat_ids[None, :]) & (
        assign_index[None, :] < assign_index[:, None]
    )
    rank_in = jnp.sum(earlier.astype(jnp.int32), axis=1)
    slot = dest * slots + rank_in[:, None]
    hits = jnp.any(
        slot[None, :, :] == jnp.arange(nreq * slots, dtype=jnp.int32)[:, None, None], axis=-1
    )
    repeated = jnp.repeat(normed.reshape(batches * tok_rows, width), topk, axis=0)
    my_half = lax.dynamic_slice_in_dim(repeated, core * half, half, 1)
    outgoing = jnp.dot(hits.astype(jnp.bfloat16), my_half, preferred_element_type=jnp.float32)
    outgoing = outgoing.astype(jnp.bfloat16).reshape(nreq, slots, half)
    received = lax.all_to_all(outgoing, "req", split_axis=0, concat_axis=0, tiled=True)
    other = lax.ppermute(received, "tp", CORE_PAIRS)
    low = jnp.where(core == 0, received, other)
    high = jnp.where(core == 0, other, received)
    flat_rows = jnp.concatenate([low, high], axis=-1).reshape(nreq * slots, width)
    gate_up = jnp.dot(
        flat_rows, shard_weights[:, : 2 * hid_dev], preferred_element_type=jnp.float32
    )
    act = (jax.nn.silu(gate_up[:, :hid_dev]) * gate_up[:, hid_dev:]).astype(jnp.bfloat16)
    part = lax.dot_general(
        act,
        shard_weights[:, 2 * hid_dev :],
        (((1,), (1,)), ((), ())),
        preferred_element_type=jnp.float32,
    ).astype(jnp.bfloat16)
    part = part.reshape(nreq * slots, 2, 2, quarter)
    keep = lax.dynamic_index_in_dim(part, core, 2, keepdims=False)
    send = lax.dynamic_index_in_dim(part, 1 - core, 2, keepdims=False)
    got = lax.ppermute(send, "tp", CORE_PAIRS)
    pair_sum = (keep.astype(jnp.float32) + got.astype(jnp.float32)).astype(jnp.bfloat16)
    pair_sum = pair_sum.reshape(nreq, slots * half)
    sending = extra.reshape(nreq, -1)
    both = lax.all_to_all(
        jnp.concatenate([pair_sum, sending], axis=1), "req", split_axis=0, concat_axis=0, tiled=True
    )
    returned = both[:, : slots * half].reshape(nreq * slots, 2, quarter)
    collected = both[:, slots * half :]
    picked = (
        returned[slot.reshape(-1)]
        .astype(jnp.float32)
        .reshape(batches * tok_rows, topk, split_count, 2, quarter)
    )
    weights_now = route_weights.reshape(batches * tok_rows, topk)
    partial_sum = jnp.einsum("rksze,rk->rze", picked, weights_now)
    mine = lax.dynamic_index_in_dim(partial_sum, zpos, 1, keepdims=False)
    away = lax.dynamic_index_in_dim(partial_sum, 1 - zpos, 1, keepdims=False)
    total = mine + lax.ppermute(away, "tp", Z_PAIRS)
    resid_share = lax.dynamic_slice_in_dim(resid, tp_index * quarter, quarter, 2)
    return (resid_share + total.reshape(batches, tok_rows, quarter)).astype(jnp.bfloat16), collected


def migrate(old_weights, old_place, new_place):
    nreq = lax.axis_size("req")
    shard_count = EXPERTS * max(1, nreq // 16)
    _, width, columns = old_weights.shape
    piece = width // nreq
    pieces = old_weights.reshape(nreq, piece, columns)
    spread = lax.all_to_all(pieces, "req", split_axis=0, concat_axis=0, tiled=True)
    devices = jnp.arange(nreq, dtype=jnp.int32)
    shard_ids = jnp.arange(shard_count, dtype=jnp.int32)
    first_old = jnp.min(
        jnp.where(old_place[None, :] == shard_ids[:, None], devices[None, :], nreq), axis=1
    )
    needed = jnp.sum(
        jnp.where(new_place[:, None] == shard_ids[None, :], first_old[None, :], 0), axis=1
    )
    return spread[needed]


def on_device(
    queries,
    new_keys,
    new_values,
    cache_keys,
    cache_values,
    lengths,
    hidden,
    gain,
    expert_ids,
    route_weights,
    old_place,
    new_place,
    old_weights,
):
    context = attend(queries, new_keys, new_values, cache_keys, cache_values, lengths)
    sending = migrate(old_weights, old_place, new_place)
    layer_out, collected = expert_routed(
        hidden, expert_ids, route_weights, old_place, old_weights[0], gain, sending
    )
    moved = collected.reshape(old_weights.shape)
    return (context, layer_out, moved)


def solution(mesh):
    in_specs = (
        P(None, "req", "tp"),
        P(None, "req", "tp"),
        P(None, "req", "tp"),
        P("req", "tp"),
        P("req", "tp"),
        P("req", None),
        P(None, "req", None),
        P(),
        P(None, "req", None),
        P(None, "req", None),
        P(),
        P(),
        P("req", None, "tp"),
    )
    out_specs = (P(None, "req", "tp"), P(None, "req", "tp"), P("req", None, "tp"))
    return jax.shard_map(
        on_device, mesh=mesh, in_specs=in_specs, out_specs=out_specs, check_vma=False
    )
```

```python
import jax
import jax.numpy as jnp
from jax import lax
from jax.sharding import PartitionSpec as P

HEAD_SIZE = 64
EXPERTS = 8
CAP = 3


def attend(queries, new_keys, new_values, cache_keys, cache_values, lengths):
    batches, tok_rows, width = queries.shape
    heads = width // HEAD_SIZE
    pool = cache_keys.shape[0]
    scale = HEAD_SIZE ** (-0.5)
    req_lengths = lengths.reshape(-1)
    starts = jnp.cumsum(req_lengths) - req_lengths
    position = jnp.arange(pool, dtype=jnp.int32)
    owned = (position[None, :] >= starts[:, None]) & (
        position[None, :] < (starts + req_lengths)[:, None]
    )
    query_rows = queries.reshape(batches * tok_rows, heads, HEAD_SIZE)
    own_keys = new_keys.reshape(batches * tok_rows, heads, HEAD_SIZE)
    own_values = new_values.reshape(batches * tok_rows, heads, HEAD_SIZE)
    pool_keys = cache_keys.reshape(pool, heads, HEAD_SIZE)
    pool_values = cache_values.reshape(pool, heads, HEAD_SIZE)
    scores = (
        jnp.einsum("qhd,phd->hqp", query_rows, pool_keys, preferred_element_type=jnp.float32)
        * scale
    )
    scores = jnp.where(owned[None], scores, -jnp.inf)
    own_score = (
        jnp.einsum("qhd,qhd->hq", query_rows, own_keys, preferred_element_type=jnp.float32) * scale
    )
    highest = jnp.maximum(jnp.max(scores, axis=-1), own_score)
    exp_pool = jnp.exp(scores - highest[..., None])
    exp_own = jnp.exp(own_score - highest)
    denom = jnp.sum(exp_pool, axis=-1) + exp_own
    summed = jnp.einsum(
        "hqp,phd->qhd",
        exp_pool.astype(jnp.bfloat16),
        pool_values,
        preferred_element_type=jnp.float32,
    )
    prob_own = lax.optimization_barrier(exp_own.astype(jnp.bfloat16)).astype(jnp.float32)
    summed = summed + prob_own.T[:, :, None] * own_values.astype(jnp.float32)
    context = (summed / denom.T[:, :, None]).astype(jnp.bfloat16)
    return context.reshape(batches, tok_rows, width)


def choose_holders(place, me_index, nreq, shard_count):
    devices = jnp.arange(nreq, dtype=jnp.int32)
    holder = place[None, :] == jnp.arange(shard_count, dtype=jnp.int32)[:, None]
    before = (place[:, None] == place[None, :]) & (devices[:, None] < devices[None, :])
    rank_in = jnp.sum(before.astype(jnp.int32), axis=0)
    count = jnp.sum(holder.astype(jnp.int32), axis=1)
    wanted = me_index % count
    match = holder & (rank_in[None, :] == wanted[:, None])
    return jnp.sum(jnp.where(match, devices[None, :], 0), axis=1)


CORE_PAIRS = [(0, 1), (1, 0), (2, 3), (3, 2)]
Z_PAIRS = [(0, 2), (2, 0), (1, 3), (3, 1)]


def expert_routed(hidden, chosen, route_weights, place, shard_weights, gain, extra):
    nreq = lax.axis_size("req")
    me_index = lax.axis_index("req")
    tp_index = lax.axis_index("tp")
    core = tp_index % 2
    zpos = tp_index // 2
    split_count = max(1, nreq // 16)
    shard_count = EXPERTS * split_count
    batches, tok_rows, width = hidden.shape
    slots = batches * CAP
    half = width // 2
    quarter = width // 4
    hid_dev = shard_weights.shape[1] // 3
    resid = hidden.astype(jnp.float32)
    normed = (
        resid * gain / jnp.sqrt(jnp.mean(resid * resid, axis=-1, keepdims=True) + 1e-05)
    ).astype(jnp.bfloat16)
    flat_ids = chosen.reshape(-1)
    assigns = flat_ids.shape[0]
    topk = assigns // (batches * tok_rows)
    shard_dest = choose_holders(place, me_index, nreq, shard_count)
    shard_list = flat_ids[:, None] * split_count + jnp.arange(split_count, dtype=jnp.int32)[None, :]
    pick = shard_list[:, :, None] == jnp.arange(shard_count, dtype=jnp.int32)[None, None, :]
    dest = jnp.sum(jnp.where(pick, shard_dest[None, None, :], 0), axis=-1)
    assign_index = jnp.arange(assigns, dtype=jnp.int32)
    earlier = (flat_ids[:, None] == flat_ids[None, :]) & (
        assign_index[None, :] < assign_index[:, None]
    )
    rank_in = jnp.sum(earlier.astype(jnp.int32), axis=1)
    slot = dest * slots + rank_in[:, None]
    hits = jnp.any(
        slot[None, :, :] == jnp.arange(nreq * slots, dtype=jnp.int32)[:, None, None], axis=-1
    )
    repeated = jnp.repeat(normed.reshape(batches * tok_rows, width), topk, axis=0)
    my_half = lax.dynamic_slice_in_dim(repeated, core * half, half, 1)
    outgoing = jnp.dot(hits.astype(jnp.bfloat16), my_half, preferred_element_type=jnp.float32)
    outgoing = outgoing.astype(jnp.bfloat16).reshape(nreq, slots, half)
    received = lax.all_to_all(outgoing, "req", split_axis=0, concat_axis=0, tiled=True)
    other = lax.ppermute(received, "tp", CORE_PAIRS)
    low = jnp.where(core == 0, received, other)
    high = jnp.where(core == 0, other, received)
    flat_rows = jnp.concatenate([low, high], axis=-1).reshape(nreq * slots, width)
    gate_up = jnp.dot(
        flat_rows, shard_weights[:, : 2 * hid_dev], preferred_element_type=jnp.float32
    )
    act = (jax.nn.silu(gate_up[:, :hid_dev]) * gate_up[:, hid_dev:]).astype(jnp.bfloat16)
    part = lax.dot_general(
        act,
        shard_weights[:, 2 * hid_dev :],
        (((1,), (1,)), ((), ())),
        preferred_element_type=jnp.float32,
    ).astype(jnp.bfloat16)
    part = part.reshape(nreq * slots, 2, 2, quarter)
    keep = lax.dynamic_index_in_dim(part, core, 2, keepdims=False)
    send = lax.dynamic_index_in_dim(part, 1 - core, 2, keepdims=False)
    got = lax.ppermute(send, "tp", CORE_PAIRS)
    pair_sum = (keep.astype(jnp.float32) + got.astype(jnp.float32)).astype(jnp.bfloat16)
    piece_rows, piece_lanes = extra.shape[1:]
    pair_sum = pair_sum.reshape(nreq, slots * half)
    pair_sum = jnp.pad(pair_sum, ((0, 0), (0, piece_rows * piece_lanes - slots * half)))
    pair_sum = pair_sum.reshape(nreq, piece_rows, piece_lanes)
    both = lax.all_to_all(
        jnp.concatenate([extra, pair_sum], axis=1), "req", split_axis=0, concat_axis=0, tiled=True
    )
    collected = both[:, :piece_rows]
    returned = both[:, piece_rows:].reshape(nreq, piece_rows * piece_lanes)[:, : slots * half]
    returned = returned.reshape(nreq * slots, 2, quarter)
    picked = (
        returned[slot.reshape(-1)]
        .astype(jnp.float32)
        .reshape(batches * tok_rows, topk, split_count, 2, quarter)
    )
    weights_now = route_weights.reshape(batches * tok_rows, topk)
    partial_sum = jnp.einsum("rksze,rk->rze", picked, weights_now)
    mine = lax.dynamic_index_in_dim(partial_sum, zpos, 1, keepdims=False)
    away = lax.dynamic_index_in_dim(partial_sum, 1 - zpos, 1, keepdims=False)
    total = mine + lax.ppermute(away, "tp", Z_PAIRS)
    resid_share = lax.dynamic_slice_in_dim(resid, tp_index * quarter, quarter, 2)
    return (resid_share + total.reshape(batches, tok_rows, quarter)).astype(jnp.bfloat16), collected


def migrate(old_weights, old_place, new_place):
    nreq = lax.axis_size("req")
    shard_count = EXPERTS * max(1, nreq // 16)
    _, width, columns = old_weights.shape
    piece = width * columns // nreq
    pieces = old_weights.reshape(nreq, 16, piece // 16)
    spread = lax.all_to_all(pieces, "req", split_axis=0, concat_axis=0, tiled=True)
    devices = jnp.arange(nreq, dtype=jnp.int32)
    shard_ids = jnp.arange(shard_count, dtype=jnp.int32)
    first_old = jnp.min(
        jnp.where(old_place[None, :] == shard_ids[:, None], devices[None, :], nreq), axis=1
    )
    needed = jnp.sum(
        jnp.where(new_place[:, None] == shard_ids[None, :], first_old[None, :], 0), axis=1
    )
    return spread[needed]


def on_device(
    queries,
    new_keys,
    new_values,
    cache_keys,
    cache_values,
    lengths,
    hidden,
    gain,
    expert_ids,
    route_weights,
    old_place,
    new_place,
    old_weights,
):
    context = attend(queries, new_keys, new_values, cache_keys, cache_values, lengths)
    sending = migrate(old_weights, old_place, new_place)
    layer_out, collected = expert_routed(
        hidden, expert_ids, route_weights, old_place, old_weights[0], gain, sending
    )
    moved = collected.reshape(old_weights.shape)
    return (context, layer_out, moved)


def solution(mesh):
    in_specs = (
        P(None, "req", "tp"),
        P(None, "req", "tp"),
        P(None, "req", "tp"),
        P("req", "tp"),
        P("req", "tp"),
        P("req", None),
        P(None, "req", None),
        P(),
        P(None, "req", None),
        P(None, "req", None),
        P(),
        P(),
        P("req", None, "tp"),
    )
    out_specs = (P(None, "req", "tp"), P(None, "req", "tp"), P("req", None, "tp"))
    return jax.shard_map(
        on_device, mesh=mesh, in_specs=in_specs, out_specs=out_specs, check_vma=False
    )
```

```python
import jax
import jax.numpy as jnp
from jax import lax
from jax.sharding import PartitionSpec as P

HEAD_SIZE = 64
EXPERTS = 8
CAP = 3
MIG_LANES = 1152


def attend(queries, new_keys, new_values, cache_keys, cache_values, lengths):
    batches, tok_rows, width = queries.shape
    heads = width // HEAD_SIZE
    pool = cache_keys.shape[0]
    scale = HEAD_SIZE ** (-0.5)
    req_lengths = lengths.reshape(-1)
    starts = jnp.cumsum(req_lengths) - req_lengths
    position = jnp.arange(pool, dtype=jnp.int32)
    owned = (position[None, :] >= starts[:, None]) & (
        position[None, :] < (starts + req_lengths)[:, None]
    )
    query_rows = queries.reshape(batches * tok_rows, heads, HEAD_SIZE)
    own_keys = new_keys.reshape(batches * tok_rows, heads, HEAD_SIZE)
    own_values = new_values.reshape(batches * tok_rows, heads, HEAD_SIZE)
    pool_keys = cache_keys.reshape(pool, heads, HEAD_SIZE)
    pool_values = cache_values.reshape(pool, heads, HEAD_SIZE)
    scores = (
        jnp.einsum("qhd,phd->hqp", query_rows, pool_keys, preferred_element_type=jnp.float32)
        * scale
    )
    scores = jnp.where(owned[None], scores, -jnp.inf)
    own_score = (
        jnp.einsum("qhd,qhd->hq", query_rows, own_keys, preferred_element_type=jnp.float32) * scale
    )
    highest = jnp.maximum(jnp.max(scores, axis=-1), own_score)
    exp_pool = jnp.exp(scores - highest[..., None])
    exp_own = jnp.exp(own_score - highest)
    denom = jnp.sum(exp_pool, axis=-1) + exp_own
    summed = jnp.einsum(
        "hqp,phd->qhd",
        exp_pool.astype(jnp.bfloat16),
        pool_values,
        preferred_element_type=jnp.float32,
    )
    prob_own = lax.optimization_barrier(exp_own.astype(jnp.bfloat16)).astype(jnp.float32)
    summed = summed + prob_own.T[:, :, None] * own_values.astype(jnp.float32)
    context = (summed / denom.T[:, :, None]).astype(jnp.bfloat16)
    return context.reshape(batches, tok_rows, width)


def choose_holders(place, me_index, nreq, shard_count):
    devices = jnp.arange(nreq, dtype=jnp.int32)
    holder = place[None, :] == jnp.arange(shard_count, dtype=jnp.int32)[:, None]
    before = (place[:, None] == place[None, :]) & (devices[:, None] < devices[None, :])
    rank_in = jnp.sum(before.astype(jnp.int32), axis=0)
    count = jnp.sum(holder.astype(jnp.int32), axis=1)
    wanted = me_index % count
    match = holder & (rank_in[None, :] == wanted[:, None])
    return jnp.sum(jnp.where(match, devices[None, :], 0), axis=1)


CORE_PAIRS = [(0, 1), (1, 0), (2, 3), (3, 2)]
Z_PAIRS = [(0, 2), (2, 0), (1, 3), (3, 1)]


def expert_routed(hidden, chosen, route_weights, place, shard_weights, gain, extra):
    nreq = lax.axis_size("req")
    me_index = lax.axis_index("req")
    tp_index = lax.axis_index("tp")
    core = tp_index % 2
    zpos = tp_index // 2
    split_count = max(1, nreq // 16)
    shard_count = EXPERTS * split_count
    batches, tok_rows, width = hidden.shape
    slots = batches * CAP
    half = width // 2
    quarter = width // 4
    hid_dev = shard_weights.shape[1] // 3
    resid = hidden.astype(jnp.float32)
    normed = (
        resid * gain / jnp.sqrt(jnp.mean(resid * resid, axis=-1, keepdims=True) + 1e-05)
    ).astype(jnp.bfloat16)
    flat_ids = chosen.reshape(-1)
    assigns = flat_ids.shape[0]
    topk = assigns // (batches * tok_rows)
    shard_dest = choose_holders(place, me_index, nreq, shard_count)
    shard_list = flat_ids[:, None] * split_count + jnp.arange(split_count, dtype=jnp.int32)[None, :]
    pick = shard_list[:, :, None] == jnp.arange(shard_count, dtype=jnp.int32)[None, None, :]
    dest = jnp.sum(jnp.where(pick, shard_dest[None, None, :], 0), axis=-1)
    assign_index = jnp.arange(assigns, dtype=jnp.int32)
    earlier = (flat_ids[:, None] == flat_ids[None, :]) & (
        assign_index[None, :] < assign_index[:, None]
    )
    rank_in = jnp.sum(earlier.astype(jnp.int32), axis=1)
    slot = dest * slots + rank_in[:, None]
    hits = jnp.any(
        slot[None, :, :] == jnp.arange(nreq * slots, dtype=jnp.int32)[:, None, None], axis=-1
    )
    repeated = jnp.repeat(normed.reshape(batches * tok_rows, width), topk, axis=0)
    my_half = lax.dynamic_slice_in_dim(repeated, core * half, half, 1)
    outgoing = jnp.dot(hits.astype(jnp.bfloat16), my_half, preferred_element_type=jnp.float32)
    outgoing = outgoing.astype(jnp.bfloat16).reshape(nreq, slots, half)
    received = lax.all_to_all(outgoing, "req", split_axis=0, concat_axis=0, tiled=True)
    other = lax.ppermute(received, "tp", CORE_PAIRS)
    low = jnp.where(core == 0, received, other)
    high = jnp.where(core == 0, other, received)
    flat_rows = jnp.concatenate([low, high], axis=-1).reshape(nreq * slots, width)
    gate_up = jnp.dot(
        flat_rows, shard_weights[:, : 2 * hid_dev], preferred_element_type=jnp.float32
    )
    act = (jax.nn.silu(gate_up[:, :hid_dev]) * gate_up[:, hid_dev:]).astype(jnp.bfloat16)
    part = lax.dot_general(
        act,
        shard_weights[:, 2 * hid_dev :],
        (((1,), (1,)), ((), ())),
        preferred_element_type=jnp.float32,
    ).astype(jnp.bfloat16)
    part = part.reshape(nreq * slots, 2, 2, quarter)
    keep = lax.dynamic_index_in_dim(part, core, 2, keepdims=False)
    send = lax.dynamic_index_in_dim(part, 1 - core, 2, keepdims=False)
    got = lax.ppermute(send, "tp", CORE_PAIRS)
    pair_sum = (keep.astype(jnp.float32) + got.astype(jnp.float32)).astype(jnp.bfloat16)
    pair_sum = pair_sum.reshape(nreq, slots, half)
    piece_rows = extra.shape[1]
    both = lax.all_to_all(
        jnp.concatenate([extra, pair_sum], axis=1), "req", split_axis=0, concat_axis=0, tiled=True
    )
    collected = both[:, :piece_rows]
    returned = both[:, piece_rows:].reshape(nreq * slots, 2, quarter)
    picked = (
        returned[slot.reshape(-1)]
        .astype(jnp.float32)
        .reshape(batches * tok_rows, topk, split_count, 2, quarter)
    )
    weights_now = route_weights.reshape(batches * tok_rows, topk)
    partial_sum = jnp.einsum("rksze,rk->rze", picked, weights_now)
    mine = lax.dynamic_index_in_dim(partial_sum, zpos, 1, keepdims=False)
    away = lax.dynamic_index_in_dim(partial_sum, 1 - zpos, 1, keepdims=False)
    total = mine + lax.ppermute(away, "tp", Z_PAIRS)
    resid_share = lax.dynamic_slice_in_dim(resid, tp_index * quarter, quarter, 2)
    return (resid_share + total.reshape(batches, tok_rows, quarter)).astype(jnp.bfloat16), collected


def migrate(old_weights, old_place, new_place):
    nreq = lax.axis_size("req")
    shard_count = EXPERTS * max(1, nreq // 16)
    _, width, columns = old_weights.shape
    piece = width * columns // nreq
    piece_rows = -(-piece // MIG_LANES)
    pieces = jnp.swapaxes(old_weights, 1, 2).reshape(nreq, piece)
    pieces = jnp.pad(pieces, ((0, 0), (0, piece_rows * MIG_LANES - piece)))
    pieces = pieces.reshape(nreq, piece_rows, MIG_LANES)
    spread = lax.all_to_all(pieces, "req", split_axis=0, concat_axis=0, tiled=True)
    devices = jnp.arange(nreq, dtype=jnp.int32)
    shard_ids = jnp.arange(shard_count, dtype=jnp.int32)
    first_old = jnp.min(
        jnp.where(old_place[None, :] == shard_ids[:, None], devices[None, :], nreq), axis=1
    )
    needed = jnp.sum(
        jnp.where(new_place[:, None] == shard_ids[None, :], first_old[None, :], 0), axis=1
    )
    return spread[needed]


def on_device(
    queries,
    new_keys,
    new_values,
    cache_keys,
    cache_values,
    lengths,
    hidden,
    gain,
    expert_ids,
    route_weights,
    old_place,
    new_place,
    old_weights,
):
    context = attend(queries, new_keys, new_values, cache_keys, cache_values, lengths)
    sending = migrate(old_weights, old_place, new_place)
    layer_out, collected = expert_routed(
        hidden, expert_ids, route_weights, old_place, old_weights[0], gain, sending
    )
    shard_size = old_weights.shape[1] * old_weights.shape[2]
    moved = collected.reshape(collected.shape[0], -1)[:, : shard_size // collected.shape[0]]
    moved = moved.reshape(1, old_weights.shape[2], old_weights.shape[1])
    moved = jnp.swapaxes(moved, 1, 2)
    return (context, layer_out, moved)


def solution(mesh):
    in_specs = (
        P(None, "req", "tp"),
        P(None, "req", "tp"),
        P(None, "req", "tp"),
        P("req", "tp"),
        P("req", "tp"),
        P("req", None),
        P(None, "req", None),
        P(),
        P(None, "req", None),
        P(None, "req", None),
        P(),
        P(),
        P("req", None, "tp"),
    )
    out_specs = (P(None, "req", "tp"), P(None, "req", "tp"), P("req", None, "tp"))
    return jax.shard_map(
        on_device, mesh=mesh, in_specs=in_specs, out_specs=out_specs, check_vma=False
    )
```

```python
import jax
import jax.numpy as jnp
from jax import lax
from jax.sharding import PartitionSpec as P

HEAD_SIZE = 64
EXPERTS = 8
CAP = 3


def attend(queries, new_keys, new_values, cache_keys, cache_values, lengths):
    batches, tok_rows, width = queries.shape
    heads = width // HEAD_SIZE
    pool = cache_keys.shape[0]
    scale = HEAD_SIZE ** (-0.5)
    req_lengths = lengths.reshape(-1)
    starts = jnp.cumsum(req_lengths) - req_lengths
    position = jnp.arange(pool, dtype=jnp.int32)
    owned = (position[None, :] >= starts[:, None]) & (
        position[None, :] < (starts + req_lengths)[:, None]
    )
    query_rows = queries.reshape(batches * tok_rows, heads, HEAD_SIZE)
    own_keys = new_keys.reshape(batches * tok_rows, heads, HEAD_SIZE)
    own_values = new_values.reshape(batches * tok_rows, heads, HEAD_SIZE)
    pool_keys = cache_keys.reshape(pool, heads, HEAD_SIZE)
    pool_values = cache_values.reshape(pool, heads, HEAD_SIZE)
    scores = (
        jnp.einsum("qhd,phd->hqp", query_rows, pool_keys, preferred_element_type=jnp.float32)
        * scale
    )
    scores = jnp.where(owned[None], scores, -jnp.inf)
    own_score = (
        jnp.einsum("qhd,qhd->hq", query_rows, own_keys, preferred_element_type=jnp.float32) * scale
    )
    highest = jnp.maximum(jnp.max(scores, axis=-1), own_score)
    exp_pool = jnp.exp(scores - highest[..., None])
    exp_own = jnp.exp(own_score - highest)
    denom = jnp.sum(exp_pool, axis=-1) + exp_own
    summed = jnp.einsum(
        "hqp,phd->qhd",
        exp_pool.astype(jnp.bfloat16),
        pool_values,
        preferred_element_type=jnp.float32,
    )
    prob_own = lax.optimization_barrier(exp_own.astype(jnp.bfloat16)).astype(jnp.float32)
    summed = summed + prob_own.T[:, :, None] * own_values.astype(jnp.float32)
    context = (summed / denom.T[:, :, None]).astype(jnp.bfloat16)
    return context.reshape(batches, tok_rows, width)


def choose_holders(place, me_index, nreq, shard_count):
    devices = jnp.arange(nreq, dtype=jnp.int32)
    holder = place[None, :] == jnp.arange(shard_count, dtype=jnp.int32)[:, None]
    before = (place[:, None] == place[None, :]) & (devices[:, None] < devices[None, :])
    rank_in = jnp.sum(before.astype(jnp.int32), axis=0)
    count = jnp.sum(holder.astype(jnp.int32), axis=1)
    wanted = me_index % count
    match = holder & (rank_in[None, :] == wanted[:, None])
    return jnp.sum(jnp.where(match, devices[None, :], 0), axis=1)


CORE_PAIRS = [(0, 1), (1, 0), (2, 3), (3, 2)]
Z_PAIRS = [(0, 2), (2, 0), (1, 3), (3, 1)]


def expert_routed(hidden, chosen, route_weights, place, shard_weights, gain, extra):
    nreq = lax.axis_size("req")
    me_index = lax.axis_index("req")
    tp_index = lax.axis_index("tp")
    core = tp_index % 2
    zpos = tp_index // 2
    split_count = max(1, nreq // 16)
    shard_count = EXPERTS * split_count
    batches, tok_rows, width = hidden.shape
    slots = batches * CAP
    half = width // 2
    quarter = width // 4
    hid_dev = shard_weights.shape[1] // 3
    resid = hidden.astype(jnp.float32)
    normed = (
        resid * gain / jnp.sqrt(jnp.mean(resid * resid, axis=-1, keepdims=True) + 1e-05)
    ).astype(jnp.bfloat16)
    flat_ids = chosen.reshape(-1)
    assigns = flat_ids.shape[0]
    topk = assigns // (batches * tok_rows)
    shard_dest = choose_holders(place, me_index, nreq, shard_count)
    shard_list = flat_ids[:, None] * split_count + jnp.arange(split_count, dtype=jnp.int32)[None, :]
    pick = shard_list[:, :, None] == jnp.arange(shard_count, dtype=jnp.int32)[None, None, :]
    dest = jnp.sum(jnp.where(pick, shard_dest[None, None, :], 0), axis=-1)
    assign_index = jnp.arange(assigns, dtype=jnp.int32)
    earlier = (flat_ids[:, None] == flat_ids[None, :]) & (
        assign_index[None, :] < assign_index[:, None]
    )
    rank_in = jnp.sum(earlier.astype(jnp.int32), axis=1)
    slot = dest * slots + rank_in[:, None]
    hits = jnp.any(
        slot[None, :, :] == jnp.arange(nreq * slots, dtype=jnp.int32)[:, None, None], axis=-1
    )
    repeated = jnp.repeat(normed.reshape(batches * tok_rows, width), topk, axis=0)
    my_quarter = lax.dynamic_slice_in_dim(repeated, tp_index * quarter, quarter, 1)
    outgoing = jnp.dot(hits.astype(jnp.bfloat16), my_quarter, preferred_element_type=jnp.float32)
    outgoing = outgoing.astype(jnp.bfloat16).reshape(nreq, slots, quarter)
    received = lax.all_to_all(outgoing, "req", split_axis=0, concat_axis=0, tiled=True)
    z_other = lax.ppermute(received, "tp", Z_PAIRS)
    own_pair = jnp.stack(
        [jnp.where(zpos == 0, received, z_other), jnp.where(zpos == 0, z_other, received)]
    )
    core_pair = lax.ppermute(own_pair, "tp", CORE_PAIRS)
    first = jnp.where(core == 0, own_pair, core_pair)
    second = jnp.where(core == 0, core_pair, own_pair)
    flat_rows = jnp.concatenate([first[0], second[0], first[1], second[1]], axis=-1)
    flat_rows = flat_rows.reshape(nreq * slots, width)
    gate_up = jnp.dot(
        flat_rows, shard_weights[:, : 2 * hid_dev], preferred_element_type=jnp.float32
    )
    act = (jax.nn.silu(gate_up[:, :hid_dev]) * gate_up[:, hid_dev:]).astype(jnp.bfloat16)
    part = lax.dot_general(
        act,
        shard_weights[:, 2 * hid_dev :],
        (((1,), (1,)), ((), ())),
        preferred_element_type=jnp.float32,
    ).astype(jnp.bfloat16)
    part = part.reshape(nreq * slots, 2, 2, quarter)
    keep = lax.dynamic_index_in_dim(part, core, 2, keepdims=False)
    send = lax.dynamic_index_in_dim(part, 1 - core, 2, keepdims=False)
    got = lax.ppermute(send, "tp", CORE_PAIRS)
    pair_sum = (keep.astype(jnp.float32) + got.astype(jnp.float32)).astype(jnp.bfloat16)
    piece_rows, piece_lanes = extra.shape[1:]
    pair_sum = pair_sum.reshape(nreq, slots * half)
    pair_sum = jnp.pad(pair_sum, ((0, 0), (0, piece_rows * piece_lanes - slots * half)))
    pair_sum = pair_sum.reshape(nreq, piece_rows, piece_lanes)
    both = lax.all_to_all(
        jnp.concatenate([extra, pair_sum], axis=1), "req", split_axis=0, concat_axis=0, tiled=True
    )
    collected = both[:, :piece_rows]
    returned = both[:, piece_rows:].reshape(nreq, piece_rows * piece_lanes)[:, : slots * half]
    returned = returned.reshape(nreq * slots, 2, quarter)
    picked = (
        returned[slot.reshape(-1)]
        .astype(jnp.float32)
        .reshape(batches * tok_rows, topk, split_count, 2, quarter)
    )
    weights_now = route_weights.reshape(batches * tok_rows, topk)
    partial_sum = jnp.einsum("rksze,rk->rze", picked, weights_now)
    mine = lax.dynamic_index_in_dim(partial_sum, zpos, 1, keepdims=False)
    away = lax.dynamic_index_in_dim(partial_sum, 1 - zpos, 1, keepdims=False)
    total = mine + lax.ppermute(away, "tp", Z_PAIRS)
    resid_share = lax.dynamic_slice_in_dim(resid, tp_index * quarter, quarter, 2)
    return (resid_share + total.reshape(batches, tok_rows, quarter)).astype(jnp.bfloat16), collected


def migrate(old_weights, old_place, new_place):
    nreq = lax.axis_size("req")
    shard_count = EXPERTS * max(1, nreq // 16)
    _, width, columns = old_weights.shape
    piece = width * columns // nreq
    pieces = old_weights.reshape(nreq, 16, piece // 16)
    spread = lax.all_to_all(pieces, "req", split_axis=0, concat_axis=0, tiled=True)
    devices = jnp.arange(nreq, dtype=jnp.int32)
    shard_ids = jnp.arange(shard_count, dtype=jnp.int32)
    first_old = jnp.min(
        jnp.where(old_place[None, :] == shard_ids[:, None], devices[None, :], nreq), axis=1
    )
    needed = jnp.sum(
        jnp.where(new_place[:, None] == shard_ids[None, :], first_old[None, :], 0), axis=1
    )
    return spread[needed]


def on_device(
    queries,
    new_keys,
    new_values,
    cache_keys,
    cache_values,
    lengths,
    hidden,
    gain,
    expert_ids,
    route_weights,
    old_place,
    new_place,
    old_weights,
):
    context = attend(queries, new_keys, new_values, cache_keys, cache_values, lengths)
    sending = migrate(old_weights, old_place, new_place)
    layer_out, collected = expert_routed(
        hidden, expert_ids, route_weights, old_place, old_weights[0], gain, sending
    )
    moved = collected.reshape(old_weights.shape)
    return (context, layer_out, moved)


def solution(mesh):
    in_specs = (
        P(None, "req", "tp"),
        P(None, "req", "tp"),
        P(None, "req", "tp"),
        P("req", "tp"),
        P("req", "tp"),
        P("req", None),
        P(None, "req", None),
        P(),
        P(None, "req", None),
        P(None, "req", None),
        P(),
        P(),
        P("req", None, "tp"),
    )
    out_specs = (P(None, "req", "tp"), P(None, "req", "tp"), P("req", None, "tp"))
    return jax.shard_map(
        on_device, mesh=mesh, in_specs=in_specs, out_specs=out_specs, check_vma=False
    )
```

```python
import jax
import jax.numpy as jnp
from jax import lax
from jax.sharding import PartitionSpec as P

HEAD_SIZE = 64
EXPERTS = 8
CAP = 3


def attend(queries, new_keys, new_values, cache_keys, cache_values, lengths):
    batches, tok_rows, width = queries.shape
    heads = width // HEAD_SIZE
    pool = cache_keys.shape[0]
    scale = HEAD_SIZE ** (-0.5)
    req_lengths = lengths.reshape(-1)
    starts = jnp.cumsum(req_lengths) - req_lengths
    position = jnp.arange(pool, dtype=jnp.int32)
    owned = (position[None, :] >= starts[:, None]) & (
        position[None, :] < (starts + req_lengths)[:, None]
    )
    query_rows = queries.reshape(batches * tok_rows, heads, HEAD_SIZE)
    own_keys = new_keys.reshape(batches * tok_rows, heads, HEAD_SIZE)
    own_values = new_values.reshape(batches * tok_rows, heads, HEAD_SIZE)
    pool_keys = cache_keys.reshape(pool, heads, HEAD_SIZE)
    pool_values = cache_values.reshape(pool, heads, HEAD_SIZE)
    scores = (
        jnp.einsum("qhd,phd->hqp", query_rows, pool_keys, preferred_element_type=jnp.float32)
        * scale
    )
    scores = jnp.where(owned[None], scores, -jnp.inf)
    own_score = (
        jnp.einsum("qhd,qhd->hq", query_rows, own_keys, preferred_element_type=jnp.float32) * scale
    )
    highest = jnp.maximum(jnp.max(scores, axis=-1), own_score)
    exp_pool = jnp.exp(scores - highest[..., None])
    exp_own = jnp.exp(own_score - highest)
    denom = jnp.sum(exp_pool, axis=-1) + exp_own
    summed = jnp.einsum(
        "hqp,phd->qhd",
        exp_pool.astype(jnp.bfloat16),
        pool_values,
        preferred_element_type=jnp.float32,
    )
    prob_own = lax.optimization_barrier(exp_own.astype(jnp.bfloat16)).astype(jnp.float32)
    summed = summed + prob_own.T[:, :, None] * own_values.astype(jnp.float32)
    context = (summed / denom.T[:, :, None]).astype(jnp.bfloat16)
    return context.reshape(batches, tok_rows, width)


def choose_holders(place, me_index, nreq, shard_count):
    devices = jnp.arange(nreq, dtype=jnp.int32)
    holder = place[None, :] == jnp.arange(shard_count, dtype=jnp.int32)[:, None]
    before = (place[:, None] == place[None, :]) & (devices[:, None] < devices[None, :])
    rank_in = jnp.sum(before.astype(jnp.int32), axis=0)
    count = jnp.sum(holder.astype(jnp.int32), axis=1)
    wanted = me_index % count
    match = holder & (rank_in[None, :] == wanted[:, None])
    return jnp.sum(jnp.where(match, devices[None, :], 0), axis=1)


CORE_PAIRS = [(0, 1), (1, 0), (2, 3), (3, 2)]
Z_PAIRS = [(0, 2), (2, 0), (1, 3), (3, 1)]


def expert_routed(hidden, chosen, route_weights, place, shard_weights, gain, extra):
    nreq = lax.axis_size("req")
    me_index = lax.axis_index("req")
    tp_index = lax.axis_index("tp")
    core = tp_index % 2
    zpos = tp_index // 2
    split_count = max(1, nreq // 16)
    shard_count = EXPERTS * split_count
    batches, tok_rows, width = hidden.shape
    slots = batches * CAP
    half = width // 2
    quarter = width // 4
    hid_dev = shard_weights.shape[1] // 3
    resid = hidden.astype(jnp.float32)
    normed = (
        resid * gain / jnp.sqrt(jnp.mean(resid * resid, axis=-1, keepdims=True) + 1e-05)
    ).astype(jnp.bfloat16)
    flat_ids = chosen.reshape(-1)
    assigns = flat_ids.shape[0]
    topk = assigns // (batches * tok_rows)
    shard_dest = choose_holders(place, me_index, nreq, shard_count)
    shard_list = flat_ids[:, None] * split_count + jnp.arange(split_count, dtype=jnp.int32)[None, :]
    pick = shard_list[:, :, None] == jnp.arange(shard_count, dtype=jnp.int32)[None, None, :]
    dest = jnp.sum(jnp.where(pick, shard_dest[None, None, :], 0), axis=-1)
    assign_index = jnp.arange(assigns, dtype=jnp.int32)
    earlier = (flat_ids[:, None] == flat_ids[None, :]) & (
        assign_index[None, :] < assign_index[:, None]
    )
    rank_in = jnp.sum(earlier.astype(jnp.int32), axis=1)
    slot = dest * slots + rank_in[:, None]
    hits = jnp.any(
        slot[None, :, :] == jnp.arange(nreq * slots, dtype=jnp.int32)[:, None, None], axis=-1
    )
    repeated = jnp.repeat(normed.reshape(batches * tok_rows, width), topk, axis=0)
    my_half = lax.dynamic_slice_in_dim(repeated, core * half, half, 1)
    outgoing = jnp.dot(hits.astype(jnp.bfloat16), my_half, preferred_element_type=jnp.float32)
    outgoing = outgoing.astype(jnp.bfloat16).reshape(nreq, slots, half)
    received = lax.all_to_all(outgoing, "req", split_axis=0, concat_axis=0, tiled=True)
    other = lax.ppermute(received, "tp", CORE_PAIRS)
    low = jnp.where(core == 0, received, other)
    high = jnp.where(core == 0, other, received)
    flat_rows = jnp.concatenate([low, high], axis=-1).reshape(nreq * slots, width)
    gate_up = jnp.dot(
        flat_rows, shard_weights[:, : 2 * hid_dev], preferred_element_type=jnp.float32
    )
    act = (jax.nn.silu(gate_up[:, :hid_dev]) * gate_up[:, hid_dev:]).astype(jnp.bfloat16)
    part = lax.dot_general(
        act,
        shard_weights[:, 2 * hid_dev :],
        (((1,), (1,)), ((), ())),
        preferred_element_type=jnp.float32,
    ).astype(jnp.bfloat16)
    part = part.reshape(nreq * slots, 2, 2, quarter)
    piece_rows, piece_lanes = extra.shape[1:]

    def to_payload(block):
        block = block.reshape(nreq, slots * half)
        block = jnp.pad(block, ((0, 0), (0, piece_rows * piece_lanes - slots * half)))
        return block.reshape(nreq, piece_rows, piece_lanes)

    keep = to_payload(lax.dynamic_index_in_dim(part, core, 2, keepdims=False))
    send = to_payload(lax.dynamic_index_in_dim(part, 1 - core, 2, keepdims=False))
    got = lax.ppermute(send, "tp", CORE_PAIRS)
    pair_sum = (keep.astype(jnp.float32) + got.astype(jnp.float32)).astype(jnp.bfloat16)
    both = lax.all_to_all(
        jnp.concatenate([extra, pair_sum], axis=1), "req", split_axis=0, concat_axis=0, tiled=True
    )
    collected = both[:, :piece_rows]
    returned = both[:, piece_rows:].reshape(nreq, piece_rows * piece_lanes)[:, : slots * half]
    returned = returned.reshape(nreq * slots, 2, quarter)
    picked = (
        returned[slot.reshape(-1)]
        .astype(jnp.float32)
        .reshape(batches * tok_rows, topk, split_count, 2, quarter)
    )
    weights_now = route_weights.reshape(batches * tok_rows, topk)
    partial_sum = jnp.einsum("rksze,rk->rze", picked, weights_now)
    mine = lax.dynamic_index_in_dim(partial_sum, zpos, 1, keepdims=False)
    away = lax.dynamic_index_in_dim(partial_sum, 1 - zpos, 1, keepdims=False)
    total = mine + lax.ppermute(away, "tp", Z_PAIRS)
    resid_share = lax.dynamic_slice_in_dim(resid, tp_index * quarter, quarter, 2)
    return (resid_share + total.reshape(batches, tok_rows, quarter)).astype(jnp.bfloat16), collected


def migrate(old_weights, old_place, new_place):
    nreq = lax.axis_size("req")
    shard_count = EXPERTS * max(1, nreq // 16)
    _, width, columns = old_weights.shape
    piece = width * columns // nreq
    pieces = old_weights.reshape(nreq, 16, piece // 16)
    spread = lax.all_to_all(pieces, "req", split_axis=0, concat_axis=0, tiled=True)
    devices = jnp.arange(nreq, dtype=jnp.int32)
    shard_ids = jnp.arange(shard_count, dtype=jnp.int32)
    first_old = jnp.min(
        jnp.where(old_place[None, :] == shard_ids[:, None], devices[None, :], nreq), axis=1
    )
    needed = jnp.sum(
        jnp.where(new_place[:, None] == shard_ids[None, :], first_old[None, :], 0), axis=1
    )
    return spread[needed]


def on_device(
    queries,
    new_keys,
    new_values,
    cache_keys,
    cache_values,
    lengths,
    hidden,
    gain,
    expert_ids,
    route_weights,
    old_place,
    new_place,
    old_weights,
):
    context = attend(queries, new_keys, new_values, cache_keys, cache_values, lengths)
    sending = migrate(old_weights, old_place, new_place)
    layer_out, collected = expert_routed(
        hidden, expert_ids, route_weights, old_place, old_weights[0], gain, sending
    )
    moved = collected.reshape(old_weights.shape)
    return (context, layer_out, moved)


def solution(mesh):
    in_specs = (
        P(None, "req", "tp"),
        P(None, "req", "tp"),
        P(None, "req", "tp"),
        P("req", "tp"),
        P("req", "tp"),
        P("req", None),
        P(None, "req", None),
        P(),
        P(None, "req", None),
        P(None, "req", None),
        P(),
        P(),
        P("req", None, "tp"),
    )
    out_specs = (P(None, "req", "tp"), P(None, "req", "tp"), P("req", None, "tp"))
    return jax.shard_map(
        on_device, mesh=mesh, in_specs=in_specs, out_specs=out_specs, check_vma=False
    )
```

```python
import jax
import jax.numpy as jnp
from jax import lax
from jax.sharding import PartitionSpec as P

HEAD_SIZE = 64
EXPERTS = 8
CAP = 3


def attend(queries, new_keys, new_values, cache_keys, cache_values, lengths):
    batches, tok_rows, width = queries.shape
    heads = width // HEAD_SIZE
    pool = cache_keys.shape[0]
    scale = HEAD_SIZE ** (-0.5)
    req_lengths = lengths.reshape(-1)
    starts = jnp.cumsum(req_lengths) - req_lengths
    position = jnp.arange(pool, dtype=jnp.int32)
    owned = (position[None, :] >= starts[:, None]) & (
        position[None, :] < (starts + req_lengths)[:, None]
    )
    query_rows = queries.reshape(batches * tok_rows, heads, HEAD_SIZE)
    own_keys = new_keys.reshape(batches * tok_rows, heads, HEAD_SIZE)
    own_values = new_values.reshape(batches * tok_rows, heads, HEAD_SIZE)
    pool_keys = cache_keys.reshape(pool, heads, HEAD_SIZE)
    pool_values = cache_values.reshape(pool, heads, HEAD_SIZE)
    scores = (
        jnp.einsum("qhd,phd->hqp", query_rows, pool_keys, preferred_element_type=jnp.float32)
        * scale
    )
    scores = jnp.where(owned[None], scores, -jnp.inf)
    own_score = (
        jnp.einsum("qhd,qhd->hq", query_rows, own_keys, preferred_element_type=jnp.float32) * scale
    )
    highest = jnp.maximum(jnp.max(scores, axis=-1), own_score)
    exp_pool = jnp.exp(scores - highest[..., None])
    exp_own = jnp.exp(own_score - highest)
    denom = jnp.sum(exp_pool, axis=-1) + exp_own
    summed = jnp.einsum(
        "hqp,phd->qhd",
        exp_pool.astype(jnp.bfloat16),
        pool_values,
        preferred_element_type=jnp.float32,
    )
    prob_own = lax.optimization_barrier(exp_own.astype(jnp.bfloat16)).astype(jnp.float32)
    summed = summed + prob_own.T[:, :, None] * own_values.astype(jnp.float32)
    context = (summed / denom.T[:, :, None]).astype(jnp.bfloat16)
    return context.reshape(batches, tok_rows, width)


def choose_holders(place, me_index, nreq, shard_count):
    devices = jnp.arange(nreq, dtype=jnp.int32)
    holder = place[None, :] == jnp.arange(shard_count, dtype=jnp.int32)[:, None]
    before = (place[:, None] == place[None, :]) & (devices[:, None] < devices[None, :])
    rank_in = jnp.sum(before.astype(jnp.int32), axis=0)
    count = jnp.sum(holder.astype(jnp.int32), axis=1)
    wanted = me_index % count
    match = holder & (rank_in[None, :] == wanted[:, None])
    return jnp.sum(jnp.where(match, devices[None, :], 0), axis=1)


CORE_PAIRS = [(0, 1), (1, 0), (2, 3), (3, 2)]
Z_PAIRS = [(0, 2), (2, 0), (1, 3), (3, 1)]


def expert_routed(hidden, chosen, route_weights, place, shard_weights, gain, extra):
    nreq = lax.axis_size("req")
    me_index = lax.axis_index("req")
    tp_index = lax.axis_index("tp")
    core = tp_index % 2
    zpos = tp_index // 2
    split_count = max(1, nreq // 16)
    shard_count = EXPERTS * split_count
    batches, tok_rows, width = hidden.shape
    slots = batches * CAP
    half = width // 2
    quarter = width // 4
    hid_dev = shard_weights.shape[1] // 3
    resid = hidden.astype(jnp.float32)
    normed = (
        resid * gain / jnp.sqrt(jnp.mean(resid * resid, axis=-1, keepdims=True) + 1e-05)
    ).astype(jnp.bfloat16)
    flat_ids = chosen.reshape(-1)
    assigns = flat_ids.shape[0]
    topk = assigns // (batches * tok_rows)
    shard_dest = choose_holders(place, me_index, nreq, shard_count)
    shard_list = flat_ids[:, None] * split_count + jnp.arange(split_count, dtype=jnp.int32)[None, :]
    pick = shard_list[:, :, None] == jnp.arange(shard_count, dtype=jnp.int32)[None, None, :]
    dest = jnp.sum(jnp.where(pick, shard_dest[None, None, :], 0), axis=-1)
    assign_index = jnp.arange(assigns, dtype=jnp.int32)
    earlier = (flat_ids[:, None] == flat_ids[None, :]) & (
        assign_index[None, :] < assign_index[:, None]
    )
    rank_in = jnp.sum(earlier.astype(jnp.int32), axis=1)
    slot = dest * slots + rank_in[:, None]
    hits = jnp.any(
        slot[None, :, :] == jnp.arange(nreq * slots, dtype=jnp.int32)[:, None, None], axis=-1
    )
    repeated = jnp.repeat(normed.reshape(batches * tok_rows, width), topk, axis=0)
    my_half = lax.dynamic_slice_in_dim(repeated, core * half, half, 1)
    outgoing = jnp.dot(hits.astype(jnp.bfloat16), my_half, preferred_element_type=jnp.float32)
    outgoing = outgoing.astype(jnp.bfloat16).reshape(nreq, slots, half)
    received = lax.all_to_all(outgoing, "req", split_axis=0, concat_axis=0, tiled=True)
    other = lax.ppermute(received, "tp", CORE_PAIRS)
    low = jnp.where(core == 0, received, other)
    high = jnp.where(core == 0, other, received)
    flat_rows = jnp.concatenate([low, high], axis=-1).reshape(nreq * slots, width)
    gate_up = jnp.dot(
        flat_rows, shard_weights[:, : 2 * hid_dev], preferred_element_type=jnp.float32
    )
    act = (jax.nn.silu(gate_up[:, :hid_dev]) * gate_up[:, hid_dev:]).astype(jnp.bfloat16)
    part = lax.dot_general(
        act,
        shard_weights[:, 2 * hid_dev :],
        (((1,), (1,)), ((), ())),
        preferred_element_type=jnp.float32,
    ).astype(jnp.bfloat16)
    part = part.reshape(nreq * slots, 2, 2, quarter)
    keep = lax.dynamic_index_in_dim(part, core, 2, keepdims=False)
    send = lax.dynamic_index_in_dim(part, 1 - core, 2, keepdims=False)
    got = lax.ppermute(send, "tp", CORE_PAIRS)
    pair_sum = (keep.astype(jnp.float32) + got.astype(jnp.float32)).astype(jnp.bfloat16)
    piece_rows, piece_lanes = extra.shape[1:]
    pair_sum = pair_sum.reshape(nreq, slots * half)
    pair_sum = jnp.pad(pair_sum, ((0, 0), (0, piece_rows * piece_lanes - slots * half)))
    pair_sum = pair_sum.reshape(nreq, piece_rows, piece_lanes)
    both = lax.all_to_all(
        jnp.concatenate([extra, pair_sum], axis=1), "req", split_axis=0, concat_axis=0, tiled=True
    )
    collected = both[:, :piece_rows]
    returned = both[:, piece_rows:].reshape(nreq, piece_rows * piece_lanes)[:, : slots * half]
    returned = returned.reshape(nreq * slots, 2, quarter)
    picked = (
        returned[slot.reshape(-1)]
        .astype(jnp.float32)
        .reshape(batches * tok_rows, topk, split_count, 2, quarter)
    )
    weights_now = route_weights.reshape(batches * tok_rows, topk)
    partial_sum = jnp.einsum("rksze,rk->rze", picked, weights_now)
    mine = lax.dynamic_index_in_dim(partial_sum, zpos, 1, keepdims=False)
    away = lax.dynamic_index_in_dim(partial_sum, 1 - zpos, 1, keepdims=False)
    total = mine + lax.ppermute(away, "tp", Z_PAIRS)
    resid_share = lax.dynamic_slice_in_dim(resid, tp_index * quarter, quarter, 2)
    return (resid_share + total.reshape(batches, tok_rows, quarter)).astype(jnp.bfloat16), collected


def migrate(old_weights, old_place, new_place):
    nreq = lax.axis_size("req")
    shard_count = EXPERTS * max(1, nreq // 16)
    _, width, columns = old_weights.shape
    piece = width * columns // nreq
    pieces = jnp.swapaxes(old_weights, 1, 2).reshape(nreq, 16, piece // 16)
    spread = lax.all_to_all(pieces, "req", split_axis=0, concat_axis=0, tiled=True)
    devices = jnp.arange(nreq, dtype=jnp.int32)
    shard_ids = jnp.arange(shard_count, dtype=jnp.int32)
    first_old = jnp.min(
        jnp.where(old_place[None, :] == shard_ids[:, None], devices[None, :], nreq), axis=1
    )
    needed = jnp.sum(
        jnp.where(new_place[:, None] == shard_ids[None, :], first_old[None, :], 0), axis=1
    )
    return spread[needed]


def on_device(
    queries,
    new_keys,
    new_values,
    cache_keys,
    cache_values,
    lengths,
    hidden,
    gain,
    expert_ids,
    route_weights,
    old_place,
    new_place,
    old_weights,
):
    context = attend(queries, new_keys, new_values, cache_keys, cache_values, lengths)
    sending = migrate(old_weights, old_place, new_place)
    layer_out, collected = expert_routed(
        hidden, expert_ids, route_weights, old_place, old_weights[0], gain, sending
    )
    moved = collected.reshape(1, old_weights.shape[2], old_weights.shape[1])
    moved = jnp.swapaxes(moved, 1, 2)
    return (context, layer_out, moved)


def solution(mesh):
    in_specs = (
        P(None, "req", "tp"),
        P(None, "req", "tp"),
        P(None, "req", "tp"),
        P("req", "tp"),
        P("req", "tp"),
        P("req", None),
        P(None, "req", None),
        P(),
        P(None, "req", None),
        P(None, "req", None),
        P(),
        P(),
        P("req", None, "tp"),
    )
    out_specs = (P(None, "req", "tp"), P(None, "req", "tp"), P("req", None, "tp"))
    return jax.shard_map(
        on_device, mesh=mesh, in_specs=in_specs, out_specs=out_specs, check_vma=False
    )
```

```python
import jax
import jax.numpy as jnp
from jax import lax
from jax.sharding import PartitionSpec as P

HEAD_SIZE = 64
EXPERTS = 8
CAP = 3


def attend(queries, new_keys, new_values, cache_keys, cache_values, lengths):
    batches, tok_rows, width = queries.shape
    heads = width // HEAD_SIZE
    pool = cache_keys.shape[0]
    scale = HEAD_SIZE ** (-0.5)
    req_lengths = lengths.reshape(-1)
    starts = jnp.cumsum(req_lengths) - req_lengths
    position = jnp.arange(pool, dtype=jnp.int32)
    owned = (position[None, :] >= starts[:, None]) & (
        position[None, :] < (starts + req_lengths)[:, None]
    )
    query_rows = queries.reshape(batches * tok_rows, heads, HEAD_SIZE)
    own_keys = new_keys.reshape(batches * tok_rows, heads, HEAD_SIZE)
    own_values = new_values.reshape(batches * tok_rows, heads, HEAD_SIZE)
    pool_keys = cache_keys.reshape(pool, heads, HEAD_SIZE)
    pool_values = cache_values.reshape(pool, heads, HEAD_SIZE)
    scores = (
        jnp.einsum("qhd,phd->hqp", query_rows, pool_keys, preferred_element_type=jnp.float32)
        * scale
    )
    scores = jnp.where(owned[None], scores, -jnp.inf)
    own_score = (
        jnp.einsum("qhd,qhd->hq", query_rows, own_keys, preferred_element_type=jnp.float32) * scale
    )
    highest = jnp.maximum(jnp.max(scores, axis=-1), own_score)
    exp_pool = jnp.exp(scores - highest[..., None])
    exp_own = jnp.exp(own_score - highest)
    denom = jnp.sum(exp_pool, axis=-1) + exp_own
    summed = jnp.einsum(
        "hqp,phd->qhd",
        exp_pool.astype(jnp.bfloat16),
        pool_values,
        preferred_element_type=jnp.float32,
    )
    prob_own = lax.optimization_barrier(exp_own.astype(jnp.bfloat16)).astype(jnp.float32)
    summed = summed + prob_own.T[:, :, None] * own_values.astype(jnp.float32)
    context = (summed / denom.T[:, :, None]).astype(jnp.bfloat16)
    return context.reshape(batches, tok_rows, width)


def choose_holders(place, me_index, nreq, shard_count):
    devices = jnp.arange(nreq, dtype=jnp.int32)
    holder = place[None, :] == jnp.arange(shard_count, dtype=jnp.int32)[:, None]
    before = (place[:, None] == place[None, :]) & (devices[:, None] < devices[None, :])
    rank_in = jnp.sum(before.astype(jnp.int32), axis=0)
    count = jnp.sum(holder.astype(jnp.int32), axis=1)
    wanted = me_index % count
    match = holder & (rank_in[None, :] == wanted[:, None])
    return jnp.sum(jnp.where(match, devices[None, :], 0), axis=1)


CORE_PAIRS = [(0, 1), (1, 0), (2, 3), (3, 2)]
Z_PAIRS = [(0, 2), (2, 0), (1, 3), (3, 1)]


def expert_routed(hidden, chosen, route_weights, place, shard_weights, gain, extra):
    nreq = lax.axis_size("req")
    me_index = lax.axis_index("req")
    tp_index = lax.axis_index("tp")
    core = tp_index % 2
    zpos = tp_index // 2
    split_count = max(1, nreq // 16)
    shard_count = EXPERTS * split_count
    batches, tok_rows, width = hidden.shape
    slots = batches * CAP
    half = width // 2
    quarter = width // 4
    hid_dev = shard_weights.shape[1] // 3
    resid = hidden.astype(jnp.float32)
    normed = (
        resid * gain / jnp.sqrt(jnp.mean(resid * resid, axis=-1, keepdims=True) + 1e-05)
    ).astype(jnp.bfloat16)
    flat_ids = chosen.reshape(-1)
    assigns = flat_ids.shape[0]
    topk = assigns // (batches * tok_rows)
    shard_dest = choose_holders(place, me_index, nreq, shard_count)
    shard_list = flat_ids[:, None] * split_count + jnp.arange(split_count, dtype=jnp.int32)[None, :]
    pick = shard_list[:, :, None] == jnp.arange(shard_count, dtype=jnp.int32)[None, None, :]
    dest = jnp.sum(jnp.where(pick, shard_dest[None, None, :], 0), axis=-1)
    assign_index = jnp.arange(assigns, dtype=jnp.int32)
    earlier = (flat_ids[:, None] == flat_ids[None, :]) & (
        assign_index[None, :] < assign_index[:, None]
    )
    rank_in = jnp.sum(earlier.astype(jnp.int32), axis=1)
    slot = dest * slots + rank_in[:, None]
    hits = jnp.any(
        slot[None, :, :] == jnp.arange(nreq * slots, dtype=jnp.int32)[:, None, None], axis=-1
    )
    repeated = jnp.repeat(normed.reshape(batches * tok_rows, width), topk, axis=0)
    my_half = lax.dynamic_slice_in_dim(repeated, core * half, half, 1)
    outgoing = jnp.dot(hits.astype(jnp.bfloat16), my_half, preferred_element_type=jnp.float32)
    outgoing = outgoing.astype(jnp.bfloat16).reshape(nreq, 16, slots * half // 16)
    received = lax.all_to_all(outgoing, "req", split_axis=0, concat_axis=0, tiled=True)
    received = received.reshape(nreq, slots, half)
    other = lax.ppermute(received, "tp", CORE_PAIRS)
    low = jnp.where(core == 0, received, other)
    high = jnp.where(core == 0, other, received)
    flat_rows = jnp.concatenate([low, high], axis=-1).reshape(nreq * slots, width)
    gate_up = jnp.dot(
        flat_rows, shard_weights[:, : 2 * hid_dev], preferred_element_type=jnp.float32
    )
    act = (jax.nn.silu(gate_up[:, :hid_dev]) * gate_up[:, hid_dev:]).astype(jnp.bfloat16)
    part = lax.dot_general(
        act,
        shard_weights[:, 2 * hid_dev :],
        (((1,), (1,)), ((), ())),
        preferred_element_type=jnp.float32,
    ).astype(jnp.bfloat16)
    part = part.reshape(nreq * slots, 2, 2, quarter)
    keep = lax.dynamic_index_in_dim(part, core, 2, keepdims=False)
    send = lax.dynamic_index_in_dim(part, 1 - core, 2, keepdims=False)
    got = lax.ppermute(send, "tp", CORE_PAIRS)
    pair_sum = (keep.astype(jnp.float32) + got.astype(jnp.float32)).astype(jnp.bfloat16)
    piece_rows, piece_lanes = extra.shape[1:]
    pair_sum = pair_sum.reshape(nreq, slots * half)
    pair_sum = jnp.pad(pair_sum, ((0, 0), (0, piece_rows * piece_lanes - slots * half)))
    pair_sum = pair_sum.reshape(nreq, piece_rows, piece_lanes)
    both = lax.all_to_all(
        jnp.concatenate([extra, pair_sum], axis=1), "req", split_axis=0, concat_axis=0, tiled=True
    )
    collected = both[:, :piece_rows]
    returned = both[:, piece_rows:].reshape(nreq, piece_rows * piece_lanes)[:, : slots * half]
    returned = returned.reshape(nreq * slots, 2, quarter)
    picked = (
        returned[slot.reshape(-1)]
        .astype(jnp.float32)
        .reshape(batches * tok_rows, topk, split_count, 2, quarter)
    )
    weights_now = route_weights.reshape(batches * tok_rows, topk)
    partial_sum = jnp.einsum("rksze,rk->rze", picked, weights_now)
    mine = lax.dynamic_index_in_dim(partial_sum, zpos, 1, keepdims=False)
    away = lax.dynamic_index_in_dim(partial_sum, 1 - zpos, 1, keepdims=False)
    total = mine + lax.ppermute(away, "tp", Z_PAIRS)
    resid_share = lax.dynamic_slice_in_dim(resid, tp_index * quarter, quarter, 2)
    return (resid_share + total.reshape(batches, tok_rows, quarter)).astype(jnp.bfloat16), collected


def migrate(old_weights, old_place, new_place):
    nreq = lax.axis_size("req")
    shard_count = EXPERTS * max(1, nreq // 16)
    _, width, columns = old_weights.shape
    piece = width * columns // nreq
    pieces = jnp.swapaxes(old_weights, 1, 2).reshape(nreq, 16, piece // 16)
    spread = lax.all_to_all(pieces, "req", split_axis=0, concat_axis=0, tiled=True)
    devices = jnp.arange(nreq, dtype=jnp.int32)
    shard_ids = jnp.arange(shard_count, dtype=jnp.int32)
    first_old = jnp.min(
        jnp.where(old_place[None, :] == shard_ids[:, None], devices[None, :], nreq), axis=1
    )
    needed = jnp.sum(
        jnp.where(new_place[:, None] == shard_ids[None, :], first_old[None, :], 0), axis=1
    )
    return spread[needed]


def on_device(
    queries,
    new_keys,
    new_values,
    cache_keys,
    cache_values,
    lengths,
    hidden,
    gain,
    expert_ids,
    route_weights,
    old_place,
    new_place,
    old_weights,
):
    context = attend(queries, new_keys, new_values, cache_keys, cache_values, lengths)
    sending = migrate(old_weights, old_place, new_place)
    layer_out, collected = expert_routed(
        hidden, expert_ids, route_weights, old_place, old_weights[0], gain, sending
    )
    moved = collected.reshape(1, old_weights.shape[2], old_weights.shape[1])
    moved = jnp.swapaxes(moved, 1, 2)
    return (context, layer_out, moved)


def solution(mesh):
    in_specs = (
        P(None, "req", "tp"),
        P(None, "req", "tp"),
        P(None, "req", "tp"),
        P("req", "tp"),
        P("req", "tp"),
        P("req", None),
        P(None, "req", None),
        P(),
        P(None, "req", None),
        P(None, "req", None),
        P(),
        P(),
        P("req", None, "tp"),
    )
    out_specs = (P(None, "req", "tp"), P(None, "req", "tp"), P("req", None, "tp"))
    return jax.shard_map(
        on_device, mesh=mesh, in_specs=in_specs, out_specs=out_specs, check_vma=False
    )
```

```python
import jax
import jax.numpy as jnp
from jax import lax
from jax.sharding import PartitionSpec as P

HEAD_SIZE = 64
EXPERTS = 8
CAP = 3


def attend(queries, new_keys, new_values, cache_keys, cache_values, lengths):
    batches, tok_rows, width = queries.shape
    heads = width // HEAD_SIZE
    pool = cache_keys.shape[0]
    scale = HEAD_SIZE ** (-0.5)
    req_lengths = lengths.reshape(-1)
    starts = jnp.cumsum(req_lengths) - req_lengths
    position = jnp.arange(pool, dtype=jnp.int32)
    owned = (position[None, :] >= starts[:, None]) & (
        position[None, :] < (starts + req_lengths)[:, None]
    )
    query_rows = queries.reshape(batches * tok_rows, heads, HEAD_SIZE)
    own_keys = new_keys.reshape(batches * tok_rows, heads, HEAD_SIZE)
    own_values = new_values.reshape(batches * tok_rows, heads, HEAD_SIZE)
    pool_keys = cache_keys.reshape(pool, heads, HEAD_SIZE)
    pool_values = cache_values.reshape(pool, heads, HEAD_SIZE)
    scores = (
        jnp.einsum("qhd,phd->hqp", query_rows, pool_keys, preferred_element_type=jnp.float32)
        * scale
    )
    scores = jnp.where(owned[None], scores, -jnp.inf)
    own_score = (
        jnp.einsum("qhd,qhd->hq", query_rows, own_keys, preferred_element_type=jnp.float32) * scale
    )
    highest = jnp.maximum(jnp.max(scores, axis=-1), own_score)
    exp_pool = jnp.exp(scores - highest[..., None])
    exp_own = jnp.exp(own_score - highest)
    denom = jnp.sum(exp_pool, axis=-1) + exp_own
    summed = jnp.einsum(
        "hqp,phd->qhd",
        exp_pool.astype(jnp.bfloat16),
        pool_values,
        preferred_element_type=jnp.float32,
    )
    prob_own = lax.optimization_barrier(exp_own.astype(jnp.bfloat16)).astype(jnp.float32)
    summed = summed + prob_own.T[:, :, None] * own_values.astype(jnp.float32)
    context = (summed / denom.T[:, :, None]).astype(jnp.bfloat16)
    return context.reshape(batches, tok_rows, width)


def choose_holders(place, me_index, nreq, shard_count):
    devices = jnp.arange(nreq, dtype=jnp.int32)
    holder = place[None, :] == jnp.arange(shard_count, dtype=jnp.int32)[:, None]
    before = (place[:, None] == place[None, :]) & (devices[:, None] < devices[None, :])
    rank_in = jnp.sum(before.astype(jnp.int32), axis=0)
    count = jnp.sum(holder.astype(jnp.int32), axis=1)
    wanted = me_index % count
    match = holder & (rank_in[None, :] == wanted[:, None])
    return jnp.sum(jnp.where(match, devices[None, :], 0), axis=1)


CORE_PAIRS = [(0, 1), (1, 0), (2, 3), (3, 2)]
Z_PAIRS = [(0, 2), (2, 0), (1, 3), (3, 1)]


def expert_routed(hidden, chosen, route_weights, place, shard_weights, gain, extra):
    nreq = lax.axis_size("req")
    me_index = lax.axis_index("req")
    tp_index = lax.axis_index("tp")
    core = tp_index % 2
    zpos = tp_index // 2
    split_count = max(1, nreq // 16)
    shard_count = EXPERTS * split_count
    batches, tok_rows, width = hidden.shape
    slots = batches * CAP
    half = width // 2
    quarter = width // 4
    hid_dev = shard_weights.shape[1] // 3
    resid = hidden.astype(jnp.float32)
    normed = (
        resid * gain / jnp.sqrt(jnp.mean(resid * resid, axis=-1, keepdims=True) + 1e-05)
    ).astype(jnp.bfloat16)
    flat_ids = chosen.reshape(-1)
    assigns = flat_ids.shape[0]
    topk = assigns // (batches * tok_rows)
    shard_dest = choose_holders(place, me_index, nreq, shard_count)
    shard_list = flat_ids[:, None] * split_count + jnp.arange(split_count, dtype=jnp.int32)[None, :]
    pick = shard_list[:, :, None] == jnp.arange(shard_count, dtype=jnp.int32)[None, None, :]
    dest = jnp.sum(jnp.where(pick, shard_dest[None, None, :], 0), axis=-1)
    assign_index = jnp.arange(assigns, dtype=jnp.int32)
    earlier = (flat_ids[:, None] == flat_ids[None, :]) & (
        assign_index[None, :] < assign_index[:, None]
    )
    rank_in = jnp.sum(earlier.astype(jnp.int32), axis=1)
    slot = dest * slots + rank_in[:, None]
    hits = jnp.any(
        slot[None, :, :] == jnp.arange(nreq * slots, dtype=jnp.int32)[:, None, None], axis=-1
    )
    repeated = jnp.repeat(normed.reshape(batches * tok_rows, width), topk, axis=0)
    my_half = lax.dynamic_slice_in_dim(repeated, core * half, half, 1)
    outgoing = jnp.dot(hits.astype(jnp.bfloat16), my_half, preferred_element_type=jnp.float32)
    pieces, needed = extra
    piece_rows, piece_lanes = pieces.shape[1:]
    outgoing = outgoing.astype(jnp.bfloat16).reshape(nreq, slots * half)
    outgoing = jnp.pad(outgoing, ((0, 0), (0, piece_rows * piece_lanes - slots * half)))
    outgoing = outgoing.reshape(nreq, piece_rows, piece_lanes)
    first = lax.all_to_all(
        jnp.concatenate([pieces, outgoing], axis=1), "req", split_axis=0, concat_axis=0, tiled=True
    )
    collected = lax.all_to_all(
        first[:, :piece_rows][needed], "req", split_axis=0, concat_axis=0, tiled=True
    )
    received = first[:, piece_rows:].reshape(nreq, piece_rows * piece_lanes)[:, : slots * half]
    received = received.reshape(nreq, slots, half)
    other = lax.ppermute(received, "tp", CORE_PAIRS)
    low = jnp.where(core == 0, received, other)
    high = jnp.where(core == 0, other, received)
    flat_rows = jnp.concatenate([low, high], axis=-1).reshape(nreq * slots, width)
    gate_up = jnp.dot(
        flat_rows, shard_weights[:, : 2 * hid_dev], preferred_element_type=jnp.float32
    )
    act = (jax.nn.silu(gate_up[:, :hid_dev]) * gate_up[:, hid_dev:]).astype(jnp.bfloat16)
    part = lax.dot_general(
        act,
        shard_weights[:, 2 * hid_dev :],
        (((1,), (1,)), ((), ())),
        preferred_element_type=jnp.float32,
    ).astype(jnp.bfloat16)
    part = part.reshape(nreq * slots, 2, 2, quarter)
    keep = lax.dynamic_index_in_dim(part, core, 2, keepdims=False)
    send = lax.dynamic_index_in_dim(part, 1 - core, 2, keepdims=False)
    got = lax.ppermute(send, "tp", CORE_PAIRS)
    pair_sum = (keep.astype(jnp.float32) + got.astype(jnp.float32)).astype(jnp.bfloat16)
    pair_sum = pair_sum.reshape(nreq, 16, slots * half // 16)
    returned = lax.all_to_all(pair_sum, "req", split_axis=0, concat_axis=0, tiled=True)
    returned = returned.reshape(nreq * slots, 2, quarter)
    picked = (
        returned[slot.reshape(-1)]
        .astype(jnp.float32)
        .reshape(batches * tok_rows, topk, split_count, 2, quarter)
    )
    weights_now = route_weights.reshape(batches * tok_rows, topk)
    partial_sum = jnp.einsum("rksze,rk->rze", picked, weights_now)
    mine = lax.dynamic_index_in_dim(partial_sum, zpos, 1, keepdims=False)
    away = lax.dynamic_index_in_dim(partial_sum, 1 - zpos, 1, keepdims=False)
    total = mine + lax.ppermute(away, "tp", Z_PAIRS)
    resid_share = lax.dynamic_slice_in_dim(resid, tp_index * quarter, quarter, 2)
    return (resid_share + total.reshape(batches, tok_rows, quarter)).astype(jnp.bfloat16), collected


def migrate(old_weights, old_place, new_place):
    nreq = lax.axis_size("req")
    shard_count = EXPERTS * max(1, nreq // 16)
    _, width, columns = old_weights.shape
    piece = width * columns // nreq
    pieces = jnp.swapaxes(old_weights, 1, 2).reshape(nreq, 16, piece // 16)
    devices = jnp.arange(nreq, dtype=jnp.int32)
    shard_ids = jnp.arange(shard_count, dtype=jnp.int32)
    first_old = jnp.min(
        jnp.where(old_place[None, :] == shard_ids[:, None], devices[None, :], nreq), axis=1
    )
    needed = jnp.sum(
        jnp.where(new_place[:, None] == shard_ids[None, :], first_old[None, :], 0), axis=1
    )
    return pieces, needed


def on_device(
    queries,
    new_keys,
    new_values,
    cache_keys,
    cache_values,
    lengths,
    hidden,
    gain,
    expert_ids,
    route_weights,
    old_place,
    new_place,
    old_weights,
):
    context = attend(queries, new_keys, new_values, cache_keys, cache_values, lengths)
    sending = migrate(old_weights, old_place, new_place)
    layer_out, collected = expert_routed(
        hidden, expert_ids, route_weights, old_place, old_weights[0], gain, sending
    )
    moved = collected.reshape(1, old_weights.shape[2], old_weights.shape[1])
    moved = jnp.swapaxes(moved, 1, 2)
    return (context, layer_out, moved)


def solution(mesh):
    in_specs = (
        P(None, "req", "tp"),
        P(None, "req", "tp"),
        P(None, "req", "tp"),
        P("req", "tp"),
        P("req", "tp"),
        P("req", None),
        P(None, "req", None),
        P(),
        P(None, "req", None),
        P(None, "req", None),
        P(),
        P(),
        P("req", None, "tp"),
    )
    out_specs = (P(None, "req", "tp"), P(None, "req", "tp"), P("req", None, "tp"))
    return jax.shard_map(
        on_device, mesh=mesh, in_specs=in_specs, out_specs=out_specs, check_vma=False
    )
```

```python
import jax
import jax.numpy as jnp
from jax import lax
from jax.sharding import PartitionSpec as P

HEAD_SIZE = 64
EXPERTS = 8
CAP = 3


def attend(queries, new_keys, new_values, cache_keys, cache_values, lengths):
    batches, tok_rows, width = queries.shape
    heads = width // HEAD_SIZE
    pool = cache_keys.shape[0]
    scale = HEAD_SIZE ** (-0.5)
    req_lengths = lengths.reshape(-1)
    starts = jnp.cumsum(req_lengths) - req_lengths
    position = jnp.arange(pool, dtype=jnp.int32)
    owned = (position[None, :] >= starts[:, None]) & (
        position[None, :] < (starts + req_lengths)[:, None]
    )
    query_rows = queries.reshape(batches * tok_rows, heads, HEAD_SIZE)
    own_keys = new_keys.reshape(batches * tok_rows, heads, HEAD_SIZE)
    own_values = new_values.reshape(batches * tok_rows, heads, HEAD_SIZE)
    pool_keys = cache_keys.reshape(pool, heads, HEAD_SIZE)
    pool_values = cache_values.reshape(pool, heads, HEAD_SIZE)
    scores = (
        jnp.einsum("qhd,phd->hqp", query_rows, pool_keys, preferred_element_type=jnp.float32)
        * scale
    )
    scores = jnp.where(owned[None], scores, -jnp.inf)
    own_score = (
        jnp.einsum("qhd,qhd->hq", query_rows, own_keys, preferred_element_type=jnp.float32) * scale
    )
    highest = jnp.maximum(jnp.max(scores, axis=-1), own_score)
    exp_pool = jnp.exp(scores - highest[..., None])
    exp_own = jnp.exp(own_score - highest)
    denom = jnp.sum(exp_pool, axis=-1) + exp_own
    summed = jnp.einsum(
        "hqp,phd->qhd",
        exp_pool.astype(jnp.bfloat16),
        pool_values,
        preferred_element_type=jnp.float32,
    )
    prob_own = lax.optimization_barrier(exp_own.astype(jnp.bfloat16)).astype(jnp.float32)
    summed = summed + prob_own.T[:, :, None] * own_values.astype(jnp.float32)
    context = (summed / denom.T[:, :, None]).astype(jnp.bfloat16)
    return context.reshape(batches, tok_rows, width)


def choose_holders(place, me_index, nreq, shard_count):
    devices = jnp.arange(nreq, dtype=jnp.int32)
    holder = place[None, :] == jnp.arange(shard_count, dtype=jnp.int32)[:, None]
    before = (place[:, None] == place[None, :]) & (devices[:, None] < devices[None, :])
    rank_in = jnp.sum(before.astype(jnp.int32), axis=0)
    count = jnp.sum(holder.astype(jnp.int32), axis=1)
    wanted = me_index % count
    match = holder & (rank_in[None, :] == wanted[:, None])
    return jnp.sum(jnp.where(match, devices[None, :], 0), axis=1)


CORE_PAIRS = [(0, 1), (1, 0), (2, 3), (3, 2)]
Z_PAIRS = [(0, 2), (2, 0), (1, 3), (3, 1)]


def expert_routed(hidden, chosen, route_weights, place, shard_weights, gain, extra):
    nreq = lax.axis_size("req")
    me_index = lax.axis_index("req")
    tp_index = lax.axis_index("tp")
    core = tp_index % 2
    zpos = tp_index // 2
    split_count = max(1, nreq // 16)
    shard_count = EXPERTS * split_count
    batches, tok_rows, width = hidden.shape
    slots = batches * CAP
    half = width // 2
    quarter = width // 4
    hid_dev = shard_weights.shape[1] // 3
    resid = hidden.astype(jnp.float32)
    normed = (
        resid * gain / jnp.sqrt(jnp.mean(resid * resid, axis=-1, keepdims=True) + 1e-05)
    ).astype(jnp.bfloat16)
    flat_ids = chosen.reshape(-1)
    assigns = flat_ids.shape[0]
    topk = assigns // (batches * tok_rows)
    shard_dest = choose_holders(place, me_index, nreq, shard_count)
    shard_list = flat_ids[:, None] * split_count + jnp.arange(split_count, dtype=jnp.int32)[None, :]
    pick = shard_list[:, :, None] == jnp.arange(shard_count, dtype=jnp.int32)[None, None, :]
    dest = jnp.sum(jnp.where(pick, shard_dest[None, None, :], 0), axis=-1)
    assign_index = jnp.arange(assigns, dtype=jnp.int32)
    earlier = (flat_ids[:, None] == flat_ids[None, :]) & (
        assign_index[None, :] < assign_index[:, None]
    )
    rank_in = jnp.sum(earlier.astype(jnp.int32), axis=1)
    slot = dest * slots + rank_in[:, None]
    hits = jnp.any(
        slot[None, :, :] == jnp.arange(nreq * slots, dtype=jnp.int32)[:, None, None], axis=-1
    )
    repeated = jnp.repeat(normed.reshape(batches * tok_rows, width), topk, axis=0)
    my_half = lax.dynamic_slice_in_dim(repeated, core * half, half, 1)
    outgoing = jnp.dot(hits.astype(jnp.bfloat16), my_half, preferred_element_type=jnp.float32)
    outgoing = outgoing.astype(jnp.bfloat16).reshape(nreq, 16, slots * half // 16)
    received = lax.all_to_all(outgoing, "req", split_axis=0, concat_axis=0, tiled=True)
    received = received.reshape(nreq, slots, half)
    other = lax.ppermute(received, "tp", CORE_PAIRS)
    low = jnp.where(core == 0, received, other)
    high = jnp.where(core == 0, other, received)
    flat_rows = jnp.concatenate([low, high], axis=-1).reshape(nreq * slots, width)
    gate_up = jnp.dot(
        flat_rows, shard_weights[:, : 2 * hid_dev], preferred_element_type=jnp.float32
    )
    act = (jax.nn.silu(gate_up[:, :hid_dev]) * gate_up[:, hid_dev:]).astype(jnp.bfloat16)
    part = lax.dot_general(
        act,
        shard_weights[:, 2 * hid_dev :],
        (((1,), (1,)), ((), ())),
        preferred_element_type=jnp.float32,
    ).astype(jnp.bfloat16)
    part = part.reshape(nreq * slots, 2, 2, quarter)
    keep = lax.dynamic_index_in_dim(part, core, 2, keepdims=False)
    send = lax.dynamic_index_in_dim(part, 1 - core, 2, keepdims=False)
    got = lax.ppermute(send, "tp", CORE_PAIRS)
    pair_sum = (keep.astype(jnp.float32) + got.astype(jnp.float32)).astype(jnp.bfloat16)
    spread, needed = extra
    pair_sum = pair_sum.reshape(nreq, 16, slots * half // 16)
    returned = lax.all_to_all(pair_sum, "req", split_axis=0, concat_axis=0, tiled=True)
    returned, spread = lax.optimization_barrier((returned, spread))
    collected = lax.all_to_all(spread[needed], "req", split_axis=0, concat_axis=0, tiled=True)
    returned = returned.reshape(nreq * slots, 2, quarter)
    picked = (
        returned[slot.reshape(-1)]
        .astype(jnp.float32)
        .reshape(batches * tok_rows, topk, split_count, 2, quarter)
    )
    weights_now = route_weights.reshape(batches * tok_rows, topk)
    partial_sum = jnp.einsum("rksze,rk->rze", picked, weights_now)
    mine = lax.dynamic_index_in_dim(partial_sum, zpos, 1, keepdims=False)
    away = lax.dynamic_index_in_dim(partial_sum, 1 - zpos, 1, keepdims=False)
    total = mine + lax.ppermute(away, "tp", Z_PAIRS)
    resid_share = lax.dynamic_slice_in_dim(resid, tp_index * quarter, quarter, 2)
    return (resid_share + total.reshape(batches, tok_rows, quarter)).astype(jnp.bfloat16), collected


def migrate(old_weights, old_place, new_place):
    nreq = lax.axis_size("req")
    shard_count = EXPERTS * max(1, nreq // 16)
    _, width, columns = old_weights.shape
    piece = width * columns // nreq
    pieces = jnp.swapaxes(old_weights, 1, 2).reshape(nreq, 16, piece // 16)
    spread = lax.all_to_all(pieces, "req", split_axis=0, concat_axis=0, tiled=True)
    devices = jnp.arange(nreq, dtype=jnp.int32)
    shard_ids = jnp.arange(shard_count, dtype=jnp.int32)
    first_old = jnp.min(
        jnp.where(old_place[None, :] == shard_ids[:, None], devices[None, :], nreq), axis=1
    )
    needed = jnp.sum(
        jnp.where(new_place[:, None] == shard_ids[None, :], first_old[None, :], 0), axis=1
    )
    return spread, needed


def on_device(
    queries,
    new_keys,
    new_values,
    cache_keys,
    cache_values,
    lengths,
    hidden,
    gain,
    expert_ids,
    route_weights,
    old_place,
    new_place,
    old_weights,
):
    context = attend(queries, new_keys, new_values, cache_keys, cache_values, lengths)
    sending = migrate(old_weights, old_place, new_place)
    layer_out, collected = expert_routed(
        hidden, expert_ids, route_weights, old_place, old_weights[0], gain, sending
    )
    moved = collected.reshape(1, old_weights.shape[2], old_weights.shape[1])
    moved = jnp.swapaxes(moved, 1, 2)
    return (context, layer_out, moved)


def solution(mesh):
    in_specs = (
        P(None, "req", "tp"),
        P(None, "req", "tp"),
        P(None, "req", "tp"),
        P("req", "tp"),
        P("req", "tp"),
        P("req", None),
        P(None, "req", None),
        P(),
        P(None, "req", None),
        P(None, "req", None),
        P(),
        P(),
        P("req", None, "tp"),
    )
    out_specs = (P(None, "req", "tp"), P(None, "req", "tp"), P("req", None, "tp"))
    return jax.shard_map(
        on_device, mesh=mesh, in_specs=in_specs, out_specs=out_specs, check_vma=False
    )
```

```python
import jax
import jax.numpy as jnp
from jax import lax
from jax.sharding import PartitionSpec as P

HEAD_SIZE = 64
EXPERTS = 8
CAP = 3


def attend(queries, new_keys, new_values, cache_keys, cache_values, lengths):
    batches, tok_rows, width = queries.shape
    heads = width // HEAD_SIZE
    pool = cache_keys.shape[0]
    scale = HEAD_SIZE ** (-0.5)
    req_lengths = lengths.reshape(-1)
    starts = jnp.cumsum(req_lengths) - req_lengths
    position = jnp.arange(pool, dtype=jnp.int32)
    owned = (position[None, :] >= starts[:, None]) & (
        position[None, :] < (starts + req_lengths)[:, None]
    )
    query_rows = queries.reshape(batches * tok_rows, heads, HEAD_SIZE)
    own_keys = new_keys.reshape(batches * tok_rows, heads, HEAD_SIZE)
    own_values = new_values.reshape(batches * tok_rows, heads, HEAD_SIZE)
    pool_keys = cache_keys.reshape(pool, heads, HEAD_SIZE)
    pool_values = cache_values.reshape(pool, heads, HEAD_SIZE)
    scores = (
        jnp.einsum("qhd,phd->hqp", query_rows, pool_keys, preferred_element_type=jnp.float32)
        * scale
    )
    scores = jnp.where(owned[None], scores, -jnp.inf)
    own_score = (
        jnp.einsum("qhd,qhd->hq", query_rows, own_keys, preferred_element_type=jnp.float32) * scale
    )
    highest = jnp.maximum(jnp.max(scores, axis=-1), own_score)
    exp_pool = jnp.exp(scores - highest[..., None])
    exp_own = jnp.exp(own_score - highest)
    denom = jnp.sum(exp_pool, axis=-1) + exp_own
    summed = jnp.einsum(
        "hqp,phd->qhd",
        exp_pool.astype(jnp.bfloat16),
        pool_values,
        preferred_element_type=jnp.float32,
    )
    prob_own = lax.optimization_barrier(exp_own.astype(jnp.bfloat16)).astype(jnp.float32)
    summed = summed + prob_own.T[:, :, None] * own_values.astype(jnp.float32)
    context = (summed / denom.T[:, :, None]).astype(jnp.bfloat16)
    return context.reshape(batches, tok_rows, width)


def choose_holders(place, me_index, nreq, shard_count):
    devices = jnp.arange(nreq, dtype=jnp.int32)
    holder = place[None, :] == jnp.arange(shard_count, dtype=jnp.int32)[:, None]
    before = (place[:, None] == place[None, :]) & (devices[:, None] < devices[None, :])
    rank_in = jnp.sum(before.astype(jnp.int32), axis=0)
    count = jnp.sum(holder.astype(jnp.int32), axis=1)
    wanted = me_index % count
    match = holder & (rank_in[None, :] == wanted[:, None])
    return jnp.sum(jnp.where(match, devices[None, :], 0), axis=1)


CORE_PAIRS = [(0, 1), (1, 0), (2, 3), (3, 2)]
Z_PAIRS = [(0, 2), (2, 0), (1, 3), (3, 1)]


def expert_routed(hidden, chosen, route_weights, place, shard_weights, gain, extra):
    nreq = lax.axis_size("req")
    me_index = lax.axis_index("req")
    tp_index = lax.axis_index("tp")
    core = tp_index % 2
    zpos = tp_index // 2
    split_count = max(1, nreq // 16)
    shard_count = EXPERTS * split_count
    batches, tok_rows, width = hidden.shape
    slots = batches * CAP
    half = width // 2
    quarter = width // 4
    hid_dev = shard_weights.shape[1] // 3
    resid = hidden.astype(jnp.float32)
    normed = (
        resid * gain / jnp.sqrt(jnp.mean(resid * resid, axis=-1, keepdims=True) + 1e-05)
    ).astype(jnp.bfloat16)
    flat_ids = chosen.reshape(-1)
    assigns = flat_ids.shape[0]
    topk = assigns // (batches * tok_rows)
    shard_dest = choose_holders(place, me_index, nreq, shard_count)
    shard_list = flat_ids[:, None] * split_count + jnp.arange(split_count, dtype=jnp.int32)[None, :]
    pick = shard_list[:, :, None] == jnp.arange(shard_count, dtype=jnp.int32)[None, None, :]
    dest = jnp.sum(jnp.where(pick, shard_dest[None, None, :], 0), axis=-1)
    assign_index = jnp.arange(assigns, dtype=jnp.int32)
    earlier = (flat_ids[:, None] == flat_ids[None, :]) & (
        assign_index[None, :] < assign_index[:, None]
    )
    rank_in = jnp.sum(earlier.astype(jnp.int32), axis=1)
    slot = dest * slots + rank_in[:, None]
    hits = jnp.any(
        slot[None, :, :] == jnp.arange(nreq * slots, dtype=jnp.int32)[:, None, None], axis=-1
    )
    repeated = jnp.repeat(normed.reshape(batches * tok_rows, width), topk, axis=0)
    my_half = lax.dynamic_slice_in_dim(repeated, core * half, half, 1)
    outgoing = jnp.dot(hits.astype(jnp.bfloat16), my_half, preferred_element_type=jnp.float32)
    outgoing = outgoing.astype(jnp.bfloat16).reshape(nreq, 16, slots * half // 16)
    received = lax.all_to_all(outgoing, "req", split_axis=0, concat_axis=0, tiled=True)
    received = received.reshape(nreq, slots, half)
    other = lax.ppermute(received, "tp", CORE_PAIRS)
    low = jnp.where(core == 0, received, other)
    high = jnp.where(core == 0, other, received)
    flat_rows = jnp.concatenate([low, high], axis=-1).reshape(nreq * slots, width)
    gate_up = jnp.dot(
        flat_rows, shard_weights[:, : 2 * hid_dev], preferred_element_type=jnp.float32
    )
    act = (jax.nn.silu(gate_up[:, :hid_dev]) * gate_up[:, hid_dev:]).astype(jnp.bfloat16)
    part = lax.dot_general(
        act,
        shard_weights[:, 2 * hid_dev :],
        (((1,), (1,)), ((), ())),
        preferred_element_type=jnp.float32,
    ).astype(jnp.bfloat16)
    part = part.reshape(nreq * slots, 2, 2, quarter)
    keep = lax.dynamic_index_in_dim(part, core, 2, keepdims=False)
    send = lax.dynamic_index_in_dim(part, 1 - core, 2, keepdims=False)
    got = lax.ppermute(send, "tp", CORE_PAIRS)
    pair_sum = (keep.astype(jnp.float32) + got.astype(jnp.float32)).astype(jnp.bfloat16)
    spread, needed = extra
    pair_sum = pair_sum.reshape(nreq, slots, half)
    returned = lax.all_to_all(pair_sum, "req", split_axis=0, concat_axis=0, tiled=True)
    returned, spread = lax.optimization_barrier((returned, spread))
    collected = lax.all_to_all(spread[needed], "req", split_axis=0, concat_axis=0, tiled=True)
    returned = returned.reshape(nreq * slots, 2, quarter)
    picked = (
        returned[slot.reshape(-1)]
        .astype(jnp.float32)
        .reshape(batches * tok_rows, topk, split_count, 2, quarter)
    )
    weights_now = route_weights.reshape(batches * tok_rows, topk)
    partial_sum = jnp.einsum("rksze,rk->rze", picked, weights_now)
    mine = lax.dynamic_index_in_dim(partial_sum, zpos, 1, keepdims=False)
    away = lax.dynamic_index_in_dim(partial_sum, 1 - zpos, 1, keepdims=False)
    total = mine + lax.ppermute(away, "tp", Z_PAIRS)
    resid_share = lax.dynamic_slice_in_dim(resid, tp_index * quarter, quarter, 2)
    return (resid_share + total.reshape(batches, tok_rows, quarter)).astype(jnp.bfloat16), collected


def migrate(old_weights, old_place, new_place):
    nreq = lax.axis_size("req")
    shard_count = EXPERTS * max(1, nreq // 16)
    _, width, columns = old_weights.shape
    piece = width * columns // nreq
    pieces = jnp.swapaxes(old_weights, 1, 2).reshape(nreq, 16, piece // 16)
    spread = lax.all_to_all(pieces, "req", split_axis=0, concat_axis=0, tiled=True)
    devices = jnp.arange(nreq, dtype=jnp.int32)
    shard_ids = jnp.arange(shard_count, dtype=jnp.int32)
    first_old = jnp.min(
        jnp.where(old_place[None, :] == shard_ids[:, None], devices[None, :], nreq), axis=1
    )
    needed = jnp.sum(
        jnp.where(new_place[:, None] == shard_ids[None, :], first_old[None, :], 0), axis=1
    )
    return spread, needed


def on_device(
    queries,
    new_keys,
    new_values,
    cache_keys,
    cache_values,
    lengths,
    hidden,
    gain,
    expert_ids,
    route_weights,
    old_place,
    new_place,
    old_weights,
):
    context = attend(queries, new_keys, new_values, cache_keys, cache_values, lengths)
    sending = migrate(old_weights, old_place, new_place)
    layer_out, collected = expert_routed(
        hidden, expert_ids, route_weights, old_place, old_weights[0], gain, sending
    )
    moved = collected.reshape(1, old_weights.shape[2], old_weights.shape[1])
    moved = jnp.swapaxes(moved, 1, 2)
    return (context, layer_out, moved)


def solution(mesh):
    in_specs = (
        P(None, "req", "tp"),
        P(None, "req", "tp"),
        P(None, "req", "tp"),
        P("req", "tp"),
        P("req", "tp"),
        P("req", None),
        P(None, "req", None),
        P(),
        P(None, "req", None),
        P(None, "req", None),
        P(),
        P(),
        P("req", None, "tp"),
    )
    out_specs = (P(None, "req", "tp"), P(None, "req", "tp"), P("req", None, "tp"))
    return jax.shard_map(
        on_device, mesh=mesh, in_specs=in_specs, out_specs=out_specs, check_vma=False
    )
```
